256 devices in a mesh: atom: 8 (over x_lo, y), tm: 32 (over z, x_hi, core).
Axes of the slice: x: 4 (x_hi: 2, x_lo: 2; x = x_hi * 2 + x_lo), y: 4, z: 8, core: 2. Of those that a mesh axis runs over, the one named last changes fastest.
Arguments:
- signal: bfloat16 [306, 32768], P(None, 'tm'), may hold values from -6 to 6
- spatial: bfloat16 [256, 306], P('atom'), may hold values from -0.3125 to 0.3125
- temporal: bfloat16 [256, 256], P('atom'), may hold values from -0.375 to 0.375
- code_values: bfloat16 [256, 32768], P('atom', 'tm'), may hold values from 0 to 2
- block_mask: int32 [256, 128], P('atom', 'tm'), may hold values 0 or 1
Outputs:
- grad_spatial: float32 [256, 306], P('atom')
- grad_temporal: float32 [256, 256], P('atom')
The draws below stay inside these ranges and needn't reach their ends.
All inputs are finite; a program needn't handle non-finite values. No bound on the sum of `block_mask` on one device may be relied on, other than what follows from the above.
Results may differ from the reference program's by a relative error of at most 0.0025.
Values may be sent and summed in bfloat16 or wider, within the bound.
No kernel may reach another device: no remote copies, remote signals or barrier semaphores. Data moves between devices by JAX's collectives and lax.ppermute only.
A program may use at most 64 MiB of HBM per device.

```python
import math
import jax
import jax.numpy as jnp
from jax import lax

K = 256
P_SIZE = 306
L = 256
TIME = 32768
NBLK = 128
N_ATOM = 8


def place_ends(drawn, own_key, smallest, largest):
    index_at = [jax.random.randint(jax.random.fold_in(own_key, axis), (), 0, length) for axis, length in enumerate(drawn.shape)]
    main_axis = drawn.shape.index(max(drawn.shape))
    beside = index_at[:main_axis] + [(index_at[main_axis] + 1) % drawn.shape[main_axis]] + index_at[main_axis + 1:]
    return drawn.at[tuple(index_at)].set(smallest).at[tuple(beside)].set(largest)


def level_of(stream_key, dims, shards, low, largest):
    level, own = 1.0, jax.random.fold_in(stream_key, 6)
    for axis_at, blocks in shards:
        draws = jnp.exp(jax.random.uniform(jax.random.fold_in(own, axis_at), (blocks,), jnp.float32, low / len(shards), largest / len(shards)))
        level = level * jnp.repeat(draws, dims[axis_at] // blocks).reshape([-1 if axis == axis_at else 1 for axis in range(len(dims))])
    return level


def gaussian(key, extent, spread, bound, cuts=(), kind=jnp.bfloat16):
    result = spread * jax.random.normal(key, extent, jnp.float32)
    if cuts:
        result = result * level_of(key, extent, cuts, -0.22, 0.18)
    return jnp.clip(result, -bound, bound).astype(kind)


def setup_inputs(seed: int = 0) -> dict:
    streams_of = jax.random.split(jax.random.key(seed), 6)
    return {
        "signal": gaussian(streams_of[0], (P_SIZE, TIME), 1.0, 6.0, ((1, 32),)),
        "spatial": gaussian(streams_of[1], (K, P_SIZE), P_SIZE ** -0.5, 0.3125, ((0, 8),)),
        "temporal": gaussian(streams_of[2], (K, L), L ** -0.5, 0.375, ((0, 8),)),
        "code_values": jnp.clip(2.0 * jax.random.uniform(streams_of[3], (K, TIME), jnp.float32) ** level_of(streams_of[3], (K, TIME), ((0, 8), (1, 32)), -0.2, 0.2), 0.0, 2.0).astype(jnp.bfloat16),
        "block_mask": place_ends((jax.random.randint(streams_of[4], (K, NBLK), 0, 3) < 1).astype(jnp.int32), jax.random.fold_in(streams_of[4], 1), 0, 1),
    }


def toeplitz(kernels):
    count, length = kernels.shape
    heads = jnp.concatenate([jnp.zeros((count, 2 * length), kernels.dtype), kernels], axis=1)
    tiled = jnp.tile(heads, (1, 2 * length))[:, :2 * length * (3 * length - 1)]
    return tiled.reshape(count, 2 * length, 3 * length - 1)[:, :, :length]

def diagonals(products):
    count, rows_all, length = products.shape
    padded = jnp.concatenate([jnp.zeros((count, rows_all, 2 * length), products.dtype), products], axis=2)
    padded = padded.reshape(count, rows_all * 3 * length)
    padded = jnp.concatenate([padded, jnp.zeros((count, rows_all), products.dtype)], axis=1)
    skewed = padded.reshape(count, rows_all, 3 * length + 1)
    return lax.optimization_barrier(jnp.sum(skewed, axis=1))[:, length:2 * length]

def windows_of(extended, length):
    count, total = extended.shape
    blocks = extended.reshape(count, total // length, length)
    return jnp.concatenate([blocks[:, :-1], blocks[:, 1:]], axis=2)

def reference(signal, spatial, temporal, code_values, block_mask):
    atoms, channels = spatial.shape
    length = temporal.shape[1]
    samples = signal.shape[1]
    nblocks = samples // length
    groups = atoms // 4
    codes = (code_values.reshape(atoms, nblocks, length) * block_mask[:, :, None].astype(code_values.dtype)).reshape(atoms, samples)
    extended = jnp.concatenate([jnp.zeros((atoms, length), codes.dtype), codes], axis=1)

    def forward_group(operands):
        ext_group, kernels = operands
        windows = windows_of(ext_group, length).astype(jnp.float32)
        matrix = toeplitz(kernels).astype(jnp.float32)
        course_group = jnp.einsum('gbm,gms->gbs', windows, matrix)
        return course_group.reshape(4, samples).astype(jnp.bfloat16)
    course = lax.map(forward_group, (extended.reshape(groups, 4, length + samples), temporal.reshape(groups, 4, length)))
    course = course.reshape(atoms, samples)
    per_device = atoms // N_ATOM

    def add_group(total, operands):
        spatial_group, course_group = operands
        part = jnp.dot(spatial_group.T, course_group, preferred_element_type=jnp.float32).astype(jnp.bfloat16)
        part = lax.optimization_barrier(part)
        return (total + part.astype(jnp.float32), None)
    model, _ = lax.scan(add_group, jnp.zeros((channels, samples), jnp.float32), (spatial.reshape(N_ATOM, per_device, channels), course.reshape(N_ATOM, per_device, samples)))
    residual = (model - signal.astype(jnp.float32)).astype(jnp.bfloat16)
    projected = jnp.dot(spatial, residual, preferred_element_type=jnp.float32).astype(jnp.bfloat16)
    factor = 1.0 / math.sqrt(samples)
    grad_spatial = lax.dot_general(course, residual, (((1,), (1,)), ((), ())), preferred_element_type=jnp.float32) * factor

    def adjoint_group(operands):
        ext_group, proj_group = operands
        windows = windows_of(ext_group, length).astype(jnp.float32)
        proj_blocks = proj_group.reshape(4, nblocks, length).astype(jnp.float32)
        products = jnp.einsum('gbm,gbs->gms', windows, proj_blocks)
        return diagonals(products)
    grad_temporal = lax.map(adjoint_group, (extended.reshape(groups, 4, length + samples), projected.reshape(groups, 4, samples)))
    grad_temporal = grad_temporal.reshape(atoms, length) * factor
    return (grad_spatial, grad_temporal)
```

```python
import math

import jax
import jax.numpy as jnp
from jax import lax
from jax.experimental import pallas as pl
from jax.experimental.pallas import tpu as pltpu
from jax.sharding import PartitionSpec as P

LANES = 128


def up(n, m):
    return -(-n // m) * m


def lower_band(size):
    rows = lax.broadcasted_iota(jnp.int32, (size, size), 0)
    cols = lax.broadcasted_iota(jnp.int32, (size, size), 1)
    return cols >= rows


def course_kernel(cv_ref, mask_ref, halo_ref, temporal_ref, spatial_ref, send_ref, xs_ref, tf_ref, cs_ref):
    copies, atoms, width = send_ref.shape
    length = temporal_ref.shape[1]
    samples = cv_ref.shape[1]
    channels = spatial_ref.shape[1]
    for j in range(length // LANES):
        xs_ref[j * atoms : (j + 1) * atoms, :] = halo_ref[:, j * LANES : (j + 1) * LANES].astype(jnp.float32)
    for b in range(samples // length):
        on = mask_ref[:, b : b + 1].astype(jnp.float32)
        block = cv_ref[:, b * length : (b + 1) * length].astype(jnp.float32) * on
        for j in range(length // LANES):
            at = (length // LANES * (b + 1) + j) * atoms
            xs_ref[at : at + atoms, :] = block[:, j * LANES : (j + 1) * LANES]
    tf_ref[...] = temporal_ref[...].astype(jnp.float32)
    band = lower_band(LANES)
    rows = samples // LANES
    for k in range(atoms):
        near = pltpu.roll(
            jnp.broadcast_to(tf_ref[k : k + 1, :LANES], (LANES, LANES)), 0, 1, stride=1, stride_axis=0
        )
        far = pltpu.roll(
            jnp.broadcast_to(tf_ref[k : k + 1, LANES:], (LANES, LANES)), 0, 1, stride=1, stride_axis=0
        )
        matrix = jnp.concatenate(
            [jnp.where(band, 0.0, far), jnp.where(band, far, near), jnp.where(band, near, 0.0)], axis=0
        ).astype(jnp.bfloat16)
        windows = jnp.concatenate(
            [xs_ref[pl.ds(j * atoms + k, rows, stride=atoms), :] for j in range(3)], axis=1
        ).astype(jnp.bfloat16)
        cs_ref[pl.ds(k, rows, stride=atoms), :] = jnp.dot(
            windows, matrix, preferred_element_type=jnp.float32
        )
    padded = jnp.concatenate(
        [spatial_ref[...], jnp.zeros((atoms, width - samples - channels), jnp.bfloat16)], axis=1
    )
    for c in range(copies):
        send_ref[c, :, samples:] = padded
    for i in range(rows):
        part = cs_ref[i * atoms : (i + 1) * atoms, :].astype(jnp.bfloat16)
        for c in range(copies):
            send_ref[c, :, i * LANES : (i + 1) * LANES] = part


def gradient_kernel(factor, all_ref, own_ref, xs_ref, signal_ref, out_ref, res_ref, pr_ref, lo_ref, hi_ref):
    groups, atoms, width = all_ref.shape
    channels, samples = signal_ref.shape
    wide = width - samples
    everything = all_ref[...].reshape(groups * atoms, width)
    model = lax.dot_general(
        everything[:, samples:],
        everything[:, :samples],
        (((0,), (0,)), ((), ())),
        preferred_element_type=jnp.float32,
    )
    res_ref[channels:, :] = jnp.zeros((wide - channels, samples), jnp.bfloat16)
    res_ref[:channels, :] = (model[:channels] - signal_ref[...].astype(jnp.float32)).astype(jnp.bfloat16)
    own = own_ref[0]
    projected = jnp.dot(own[:, samples:], res_ref[...], preferred_element_type=jnp.float32)
    out_ref[:, :wide] = factor * lax.dot_general(
        own[:, :samples], res_ref[...], (((1,), (1,)), ((), ())), preferred_element_type=jnp.float32
    )
    rows = samples // LANES
    for i in range(rows):
        pr_ref[i * atoms : (i + 1) * atoms, :] = projected[:, i * LANES : (i + 1) * LANES]
    band = lower_band(LANES)
    for k in range(atoms):
        proj = pr_ref[pl.ds(k, rows, stride=atoms), :].astype(jnp.bfloat16)
        windows = jnp.concatenate(
            [xs_ref[pl.ds(j * atoms + k, rows, stride=atoms), :] for j in range(3)], axis=1
        ).astype(jnp.bfloat16)
        products = lax.dot_general(
            windows, proj, (((0,), (0,)), ((), ())), preferred_element_type=jnp.float32
        )
        old, mid, new = products[:LANES], products[LANES : 2 * LANES], products[2 * LANES :]
        for ref, total in ((lo_ref, jnp.where(band, new, mid)), (hi_ref, jnp.where(band, mid, old))):
            parts = [total[:8]]
            for a in range(1, LANES // 8):
                parts.append(pltpu.roll(total[8 * a : 8 * a + 8], LANES - 8 * a, 1))
            while len(parts) > 1:
                parts = [x + y for x, y in zip(parts[::2], parts[1::2], strict=True)]
            ref[8 * k : 8 * k + 8, :] = parts[0]
    row = lax.broadcasted_iota(jnp.int32, (8 * atoms, LANES), 0)
    for at, ref in ((wide, lo_ref), (wide + LANES, hi_ref)):
        total = ref[...]
        for bit in (1, 2, 4):
            total = jnp.where((row & bit) != 0, pltpu.roll(total, LANES - bit, 1), total)
        out_ref[:, at : at + LANES] = factor * total.reshape(atoms, 8, LANES).sum(axis=1)


def local(signal, spatial, temporal, code_values, block_mask):
    atoms, channels = spatial.shape
    length = temporal.shape[1]
    samples = signal.shape[1]
    groups, slabs = lax.axis_size("atom"), lax.axis_size("tm")
    rows = samples // LANES
    wide = up(channels, LANES)
    factor = 1.0 / math.sqrt(samples * slabs)

    tail = code_values[:, samples - length :] * block_mask[:, -1:].astype(code_values.dtype)
    halo = lax.ppermute(tail, "tm", [(i, i + 1) for i in range(slabs - 1)])
    send, xs = pl.pallas_call(
        course_kernel,
        out_shape=(
            jax.ShapeDtypeStruct((groups, atoms, samples + wide), jnp.bfloat16),
            jax.ShapeDtypeStruct(((rows + length // LANES) * atoms, LANES), jnp.float32),
        ),
        scratch_shapes=[
            pltpu.VMEM((atoms, length), jnp.float32),
            pltpu.VMEM((rows * atoms, LANES), jnp.float32),
        ],
        compiler_params=pltpu.CompilerParams(vmem_limit_bytes=32 << 20),
        name="course",
    )(code_values, block_mask, halo, temporal, spatial)
    everything = lax.all_to_all(send, "atom", split_axis=0, concat_axis=0, tiled=True)
    part = pl.pallas_call(
        lambda *refs: gradient_kernel(factor, *refs),
        grid=(1,),
        in_specs=[
            pl.BlockSpec(everything.shape, lambda i: (0, 0, 0)),
            pl.BlockSpec((1, *send.shape[1:]), lambda i: (0, 0, 0)),
            pl.BlockSpec(xs.shape, lambda i: (0, 0)),
            pl.BlockSpec(signal.shape, lambda i: (0, 0)),
        ],
        out_specs=pl.BlockSpec((atoms, wide + length), lambda i: (0, 0)),
        out_shape=jax.ShapeDtypeStruct((atoms, wide + length), jnp.float32),
        scratch_shapes=[
            pltpu.VMEM((wide, samples), jnp.bfloat16),
            pltpu.VMEM((rows * atoms, LANES), jnp.float32),
            pltpu.VMEM((8 * atoms, LANES), jnp.float32),
            pltpu.VMEM((8 * atoms, LANES), jnp.float32),
        ],
        compiler_params=pltpu.CompilerParams(vmem_limit_bytes=32 << 20),
        name="gradients",
    )(everything, send, xs, signal)
    bit = 1
    while bit < slabs:
        part = part + lax.ppermute(part, "tm", [(i, i ^ bit) for i in range(slabs)])
        bit *= 2
    return (part[:, :channels], part[:, wide:])


def solution(mesh):
    in_specs = (P(None, "tm"), P("atom", None), P("atom", None), P("atom", "tm"), P("atom", "tm"))
    out_specs = (P("atom", None), P("atom", None))
    return jax.shard_map(local, mesh=mesh, in_specs=in_specs, out_specs=out_specs, check_vma=False)
```

```python
import math

import jax
import jax.numpy as jnp
from jax import lax
from jax.experimental import pallas as pl
from jax.experimental.pallas import tpu as pltpu
from jax.sharding import PartitionSpec as P

LANES = 128
HALF = LANES // 2
PARTNERS = (2, 4, 8, 24)
VMEM_BYTES = 16 << 20


def up(n, m):
    return -(-n // m) * m


def lower_band(size):
    rows = lax.broadcasted_iota(jnp.int32, (size, size), 0)
    cols = lax.broadcasted_iota(jnp.int32, (size, size), 1)
    return cols >= rows


def codes_kernel(cv_ref, mask_ref, tail_ref, own_ref):
    atoms, samples = cv_ref.shape
    length = tail_ref.shape[1]
    per = length // LANES
    for b in reversed(range(samples // length)):
        on = mask_ref[:, b : b + 1].astype(jnp.float32)
        block = cv_ref[:, b * length : (b + 1) * length].astype(jnp.float32) * on
        if (b + 1) * length == samples:
            tail_ref[...] = block.astype(jnp.bfloat16)
        for j in range(per):
            at = (per * b + j) * atoms
            own_ref[at : at + atoms, :] = block[:, j * LANES : (j + 1) * LANES]


def course_kernel(
    own_ref, halo_ref, temporal_ref, spatial_ref, send_ref, xs_ref, tf_ref, cs_ref
):
    copies, atoms, width = send_ref.shape
    length = temporal_ref.shape[1]
    channels = spatial_ref.shape[1]
    rows = own_ref.shape[0] // atoms
    samples = rows * LANES
    per = length // LANES
    for j in range(per):
        xs_ref[j * atoms : (j + 1) * atoms, :] = halo_ref[
            :, j * LANES : (j + 1) * LANES
        ].astype(jnp.float32)
    xs_ref[per * atoms :, :] = own_ref[...]
    tf_ref[...] = temporal_ref[...].astype(jnp.float32)
    band = lower_band(LANES)

    def turned(k, at):
        row = tf_ref[k : k + 1, at : at + LANES]
        return pltpu.roll(
            jnp.broadcast_to(row, (LANES, LANES)), 0, 1, stride=1, stride_axis=0
        )

    for k in range(atoms):
        near, far = turned(k, 0), turned(k, LANES)
        matrix = jnp.concatenate(
            [jnp.where(band, 0.0, far), jnp.where(band, far, near), jnp.where(band, near, 0.0)],
            axis=0,
        ).astype(jnp.bfloat16)
        windows = jnp.concatenate(
            [xs_ref[pl.ds(j * atoms + k, rows, stride=atoms), :] for j in range(per + 1)],
            axis=1,
        ).astype(jnp.bfloat16)
        cs_ref[pl.ds(k, rows, stride=atoms), :] = jnp.dot(
            windows, matrix, preferred_element_type=jnp.float32
        )
    padded = jnp.concatenate(
        [spatial_ref[...], jnp.zeros((atoms, width - samples - channels), jnp.bfloat16)],
        axis=1,
    )
    for c in range(copies):
        send_ref[c, :, samples:] = padded
    for i in range(rows):
        part = cs_ref[i * atoms : (i + 1) * atoms, :].astype(jnp.bfloat16)
        for c in range(copies):
            send_ref[c, :, i * LANES : (i + 1) * LANES] = part


def gradient_kernel(
    factor, all_ref, own_ref, xs_ref, signal_ref, mine_ref, other_ref, res_ref, pr_ref, lo_ref, hi_ref, full_ref
):
    groups, atoms, width = all_ref.shape
    channels, samples = signal_ref.shape
    wide = width - samples
    everything = all_ref[...].reshape(groups * atoms, width)
    model = lax.dot_general(
        everything[:, samples:],
        everything[:, :samples],
        (((0,), (0,)), ((), ())),
        preferred_element_type=jnp.float32,
    )
    res_ref[channels:, :] = jnp.zeros((wide - channels, samples), jnp.bfloat16)
    res_ref[:channels, :] = (model[:channels] - signal_ref[...].astype(jnp.float32)).astype(
        jnp.bfloat16
    )
    own = own_ref[0]
    projected = jnp.dot(own[:, samples:], res_ref[...], preferred_element_type=jnp.float32)
    by_channel = factor * lax.dot_general(
        own[:, :samples], res_ref[...], (((1,), (1,)), ((), ())), preferred_element_type=jnp.float32
    )
    rows = samples // LANES
    for i in range(rows):
        pr_ref[i * atoms : (i + 1) * atoms, :] = projected[:, i * LANES : (i + 1) * LANES]
    band = lower_band(LANES)
    for k in range(atoms):
        proj = pr_ref[pl.ds(k, rows, stride=atoms), :].astype(jnp.bfloat16)
        windows = jnp.concatenate(
            [xs_ref[pl.ds(j * atoms + k, rows, stride=atoms), :] for j in range(3)], axis=1
        ).astype(jnp.bfloat16)
        products = lax.dot_general(
            windows, proj, (((0,), (0,)), ((), ())), preferred_element_type=jnp.float32
        )
        old, mid, new = products[:LANES], products[LANES : 2 * LANES], products[2 * LANES :]
        for ref, total in (
            (lo_ref, jnp.where(band, new, mid)),
            (hi_ref, jnp.where(band, mid, old)),
        ):
            parts = [total[:8]]
            for a in range(1, LANES // 8):
                parts.append(pltpu.roll(total[8 * a : 8 * a + 8], LANES - 8 * a, 1))
            while len(parts) > 1:
                parts = [x + y for x, y in zip(parts[::2], parts[1::2], strict=True)]
            ref[8 * k : 8 * k + 8, :] = parts[0]
    row = lax.broadcasted_iota(jnp.int32, (8 * atoms, LANES), 0)
    by_lag = []
    for ref in (lo_ref, hi_ref):
        total = ref[...]
        for bit in (1, 2, 4):
            total = jnp.where((row & bit) != 0, pltpu.roll(total, LANES - bit, 1), total)
        by_lag.append(factor * total.reshape(atoms, 8, LANES).sum(axis=1))
    half = atoms // 2
    lane = lax.broadcasted_iota(jnp.int32, (half // 2, LANES), 1)
    for h in range(2):
        at = h * mine_ref.shape[0]
        tiles = [by_channel[:, :LANES], by_channel[:, LANES : 2 * LANES], *by_lag]
        for t, tile in enumerate(tiles):
            full_ref[at + t * half : at + (t + 1) * half, :] = tile[h * half : (h + 1) * half]
        rest = by_channel[h * half : (h + 1) * half, 2 * LANES :]
        full_ref[at + 4 * half : at + 4 * half + half // 2, :] = jnp.where(
            lane < HALF, rest[: half // 2], pltpu.roll(rest[half // 2 :], HALF, 1)
        )
    size = mine_ref.shape[0]
    core = lax.axis_index("tm") % 2
    mine_ref[...] = full_ref[pl.ds(pl.multiple_of(core * size, 8), size), :]
    other_ref[...] = full_ref[pl.ds(pl.multiple_of((1 - core) * size, 8), size), :]


def outputs_kernel(mine_ref, other_ref, space_ref, time_ref):
    half = space_ref.shape[0] // 2
    channels = space_ref.shape[1]
    core = lax.axis_index("tm") % 2
    for ref, which in ((mine_ref, core), (other_ref, 1 - core)):
        at = pl.multiple_of(which * half, 8)
        tile = [ref[t * half : (t + 1) * half, :] for t in range(4)]
        space_ref[pl.ds(at, half), :LANES] = tile[0]
        space_ref[pl.ds(at, half), LANES : 2 * LANES] = tile[1]
        time_ref[pl.ds(at, half), :LANES] = tile[2]
        time_ref[pl.ds(at, half), LANES:] = tile[3]
        rest = ref[4 * half :, :]
        both = jnp.concatenate([rest, pltpu.roll(rest, HALF, 1)], axis=0)
        space_ref[pl.ds(at, half), 2 * LANES :] = both[:, : channels - 2 * LANES]


def local(signal, spatial, temporal, code_values, block_mask):
    atoms, channels = spatial.shape
    length = temporal.shape[1]
    samples = signal.shape[1]
    groups, slabs = lax.axis_size("atom"), lax.axis_size("tm")
    rows = samples // LANES
    wide = up(channels, LANES)
    factor = 1.0 / math.sqrt(samples * slabs)
    params = pltpu.CompilerParams(vmem_limit_bytes=VMEM_BYTES)

    def swapped(value, bit):
        return lax.ppermute(value, "tm", [(i, i ^ bit) for i in range(slabs)])

    tail, codes = pl.pallas_call(
        codes_kernel,
        out_shape=(
            jax.ShapeDtypeStruct((atoms, length), jnp.bfloat16),
            jax.ShapeDtypeStruct((rows * atoms, LANES), jnp.float32),
        ),
        compiler_params=params,
        name="codes",
    )(code_values, block_mask)
    halo = lax.ppermute(tail, "tm", [(i, i + 1) for i in range(slabs - 1)])
    send, xs = pl.pallas_call(
        course_kernel,
        out_shape=(
            jax.ShapeDtypeStruct((groups, atoms, samples + wide), jnp.bfloat16),
            jax.ShapeDtypeStruct(((rows + length // LANES) * atoms, LANES), jnp.float32),
        ),
        scratch_shapes=[
            pltpu.VMEM((atoms, length), jnp.float32),
            pltpu.VMEM((rows * atoms, LANES), jnp.float32),
        ],
        compiler_params=params,
        name="course",
    )(codes, halo, temporal, spatial)
    everything = lax.all_to_all(send, "atom", split_axis=0, concat_axis=0, tiled=True)
    size = atoms // 2 * 4 + atoms // 4
    share = jax.ShapeDtypeStruct((size, LANES), jnp.float32)
    mine, other = pl.pallas_call(
        lambda *refs: gradient_kernel(factor, *refs),
        out_shape=(share, share),
        scratch_shapes=[
            pltpu.VMEM((wide, samples), jnp.bfloat16),
            pltpu.VMEM((rows * atoms, LANES), jnp.float32),
            pltpu.VMEM((8 * atoms, LANES), jnp.float32),
            pltpu.VMEM((8 * atoms, LANES), jnp.float32),
            pltpu.VMEM((2 * size, LANES), jnp.float32),
        ],
        compiler_params=params,
        name="gradients",
    )(everything, send, xs, signal)
    mine = mine + swapped(other, 1)
    for bit in PARTNERS:
        mine = mine + swapped(mine, bit)
    return pl.pallas_call(
        outputs_kernel,
        out_shape=(
            jax.ShapeDtypeStruct((atoms, channels), jnp.float32),
            jax.ShapeDtypeStruct((atoms, length), jnp.float32),
        ),
        compiler_params=params,
        name="outputs",
    )(mine, swapped(mine, 1))


def solution(mesh):
    in_specs = (P(None, "tm"), P("atom", None), P("atom", None), P("atom", "tm"), P("atom", "tm"))
    out_specs = (P("atom", None), P("atom", None))
    return jax.shard_map(local, mesh=mesh, in_specs=in_specs, out_specs=out_specs, check_vma=False)
```

```python
import math

import jax
import jax.numpy as jnp
from jax import lax
from jax.experimental import pallas as pl
from jax.experimental.pallas import tpu as pltpu
from jax.sharding import PartitionSpec as P

LANES = 128
HALF = LANES // 2
PARTNERS = (2, 4, 8, 28)
VMEM_BYTES = 16 << 20


def up(n, m):
    return -(-n // m) * m


def lower_band(size):
    rows = lax.broadcasted_iota(jnp.int32, (size, size), 0)
    cols = lax.broadcasted_iota(jnp.int32, (size, size), 1)
    return cols >= rows


def codes_kernel(cv_ref, mask_ref, tail_ref, own_ref):
    atoms, samples = cv_ref.shape
    length = tail_ref.shape[1]
    per = length // LANES
    down = lax.broadcasted_iota(jnp.int32, (atoms, atoms), 0)
    along = lax.broadcasted_iota(jnp.int32, (atoms, atoms), 1)
    for b in reversed(range(samples // length)):
        across = jnp.broadcast_to(mask_ref[b : b + 1, :], (atoms, atoms))
        on = jnp.sum(jnp.where(down == along, across, 0).astype(jnp.float32), axis=1, keepdims=True)
        block = cv_ref[:, b * length : (b + 1) * length].astype(jnp.float32) * on
        if (b + 1) * length == samples:
            tail_ref[...] = block.astype(jnp.bfloat16)
        for j in range(per):
            at = (per * b + j) * atoms
            own_ref[at : at + atoms, :] = block[:, j * LANES : (j + 1) * LANES]


def course_kernel(
    own_ref, halo_ref, temporal_ref, spatial_ref, send_ref, xs_ref, tf_ref, cs_ref
):
    copies, atoms, width = send_ref.shape
    length = temporal_ref.shape[1]
    channels = spatial_ref.shape[1]
    rows = own_ref.shape[0] // atoms
    samples = rows * LANES
    per = length // LANES
    for j in range(per):
        xs_ref[j * atoms : (j + 1) * atoms, :] = halo_ref[
            :, j * LANES : (j + 1) * LANES
        ].astype(jnp.float32)
    xs_ref[per * atoms :, :] = own_ref[...]
    tf_ref[...] = temporal_ref[...].astype(jnp.float32)
    band = lower_band(LANES)

    def turned(k, at):
        row = tf_ref[k : k + 1, at : at + LANES]
        return pltpu.roll(
            jnp.broadcast_to(row, (LANES, LANES)), 0, 1, stride=1, stride_axis=0
        )

    for k in range(atoms):
        near, far = turned(k, 0), turned(k, LANES)
        matrix = jnp.concatenate(
            [jnp.where(band, 0.0, far), jnp.where(band, far, near), jnp.where(band, near, 0.0)],
            axis=0,
        ).astype(jnp.bfloat16)
        windows = jnp.concatenate(
            [xs_ref[pl.ds(j * atoms + k, rows, stride=atoms), :] for j in range(per + 1)],
            axis=1,
        ).astype(jnp.bfloat16)
        cs_ref[pl.ds(k, rows, stride=atoms), :] = jnp.dot(
            windows, matrix, preferred_element_type=jnp.float32
        )
    padded = jnp.concatenate(
        [spatial_ref[...], jnp.zeros((atoms, width - samples - channels), jnp.bfloat16)],
        axis=1,
    )
    for c in range(copies):
        send_ref[c, :, samples:] = padded
    for i in range(rows):
        part = cs_ref[i * atoms : (i + 1) * atoms, :].astype(jnp.bfloat16)
        for c in range(copies):
            send_ref[c, :, i * LANES : (i + 1) * LANES] = part


def gradient_kernel(
    factor, all_ref, own_ref, xs_ref, signal_ref, mine_ref, other_ref, res_ref, pr_ref, lo_ref, hi_ref, full_ref, turned_ref
):
    groups, atoms, width = all_ref.shape
    channels, samples = signal_ref.shape
    wide = width - samples
    everything = all_ref[...].reshape(groups * atoms, width)
    model = lax.dot_general(
        everything[:, samples:],
        everything[:, :samples],
        (((0,), (0,)), ((), ())),
        preferred_element_type=jnp.float32,
    )
    res_ref[channels:, :] = jnp.zeros((wide - channels, samples), jnp.bfloat16)
    res_ref[:channels, :] = (model[:channels] - signal_ref[...].astype(jnp.float32)).astype(
        jnp.bfloat16
    )
    own = own_ref[0]
    projected = jnp.dot(own[:, samples:], res_ref[...], preferred_element_type=jnp.float32)
    by_channel = factor * lax.dot_general(
        own[:, :samples], res_ref[...], (((1,), (1,)), ((), ())), preferred_element_type=jnp.float32
    )
    rows = samples // LANES
    for i in range(rows):
        pr_ref[i * atoms : (i + 1) * atoms, :] = projected[:, i * LANES : (i + 1) * LANES]
    band = lower_band(LANES)
    group = LANES // rows
    for k in range(atoms):
        if k % group == 0:
            turned = []
            for j in range(3):
                stacked = jnp.concatenate(
                    [
                        xs_ref[pl.ds(j * atoms + k + g, rows, stride=atoms), :]
                        for g in range(group)
                    ],
                    axis=0,
                )
                turned.append(stacked.T.astype(jnp.bfloat16))
            turned_ref[...] = jnp.concatenate(turned, axis=0)
        proj = pr_ref[pl.ds(k, rows, stride=atoms), :]
        above, below = (k % group) * rows, LANES - (k % group + 1) * rows
        placed = [proj]
        if above:
            placed.insert(0, jnp.zeros((above, LANES), jnp.float32))
        if below:
            placed.append(jnp.zeros((below, LANES), jnp.float32))
        products = jnp.dot(
            turned_ref[...],
            jnp.concatenate(placed, axis=0).astype(jnp.bfloat16),
            preferred_element_type=jnp.float32,
        )
        old, mid, new = products[:LANES], products[LANES : 2 * LANES], products[2 * LANES :]
        for ref, total in (
            (lo_ref, jnp.where(band, new, mid)),
            (hi_ref, jnp.where(band, mid, old)),
        ):
            parts = [total[:8]]
            for a in range(1, LANES // 8):
                parts.append(pltpu.roll(total[8 * a : 8 * a + 8], LANES - 8 * a, 1))
            while len(parts) > 1:
                parts = [x + y for x, y in zip(parts[::2], parts[1::2], strict=True)]
            ref[8 * k : 8 * k + 8, :] = parts[0]
    row = lax.broadcasted_iota(jnp.int32, (8 * atoms, LANES), 0)
    by_lag = []
    for ref in (lo_ref, hi_ref):
        total = ref[...]
        for bit in (1, 2, 4):
            total = jnp.where((row & bit) != 0, pltpu.roll(total, LANES - bit, 1), total)
        by_lag.append(factor * total.reshape(atoms, 8, LANES).sum(axis=1))
    half = atoms // 2
    lane = lax.broadcasted_iota(jnp.int32, (half // 2, LANES), 1)
    for h in range(2):
        at = h * mine_ref.shape[0]
        tiles = [by_channel[:, :LANES], by_channel[:, LANES : 2 * LANES], *by_lag]
        for t, tile in enumerate(tiles):
            full_ref[at + t * half : at + (t + 1) * half, :] = tile[h * half : (h + 1) * half]
        rest = by_channel[h * half : (h + 1) * half, 2 * LANES :]
        full_ref[at + 4 * half : at + 4 * half + half // 2, :] = jnp.where(
            lane < HALF, rest[: half // 2], pltpu.roll(rest[half // 2 :], HALF, 1)
        )
    size = mine_ref.shape[0]
    core = lax.axis_index("tm") % 2
    mine_ref[...] = full_ref[pl.ds(pl.multiple_of(core * size, 8), size), :]
    other_ref[...] = full_ref[pl.ds(pl.multiple_of((1 - core) * size, 8), size), :]


def outputs_kernel(mine_ref, other_ref, space_ref, time_ref):
    half = space_ref.shape[0] // 2
    channels = space_ref.shape[1]
    core = lax.axis_index("tm") % 2
    for ref, which in ((mine_ref, core), (other_ref, 1 - core)):
        at = pl.multiple_of(which * half, 8)
        tile = [ref[t * half : (t + 1) * half, :] for t in range(4)]
        space_ref[pl.ds(at, half), :LANES] = tile[0]
        space_ref[pl.ds(at, half), LANES : 2 * LANES] = tile[1]
        time_ref[pl.ds(at, half), :LANES] = tile[2]
        time_ref[pl.ds(at, half), LANES:] = tile[3]
        rest = ref[4 * half :, :]
        both = jnp.concatenate([rest, pltpu.roll(rest, HALF, 1)], axis=0)
        space_ref[pl.ds(at, half), 2 * LANES :] = both[:, : channels - 2 * LANES]


def local(signal, spatial, temporal, code_values, block_mask):
    atoms, channels = spatial.shape
    length = temporal.shape[1]
    samples = signal.shape[1]
    groups, slabs = lax.axis_size("atom"), lax.axis_size("tm")
    rows = samples // LANES
    wide = up(channels, LANES)
    factor = 1.0 / math.sqrt(samples * slabs)
    params = pltpu.CompilerParams(vmem_limit_bytes=VMEM_BYTES)

    def swapped(value, bit):
        return lax.ppermute(value, "tm", [(i, i ^ bit) for i in range(slabs)])

    tail, codes = pl.pallas_call(
        codes_kernel,
        out_shape=(
            jax.ShapeDtypeStruct((atoms, length), jnp.bfloat16),
            jax.ShapeDtypeStruct((rows * atoms, LANES), jnp.float32),
        ),
        compiler_params=params,
        name="codes",
    )(code_values, block_mask.T)
    halo = lax.ppermute(tail, "tm", [(i, i + 1) for i in range(slabs - 1)])
    send, xs = pl.pallas_call(
        course_kernel,
        out_shape=(
            jax.ShapeDtypeStruct((groups, atoms, samples + wide), jnp.bfloat16),
            jax.ShapeDtypeStruct(((rows + length // LANES) * atoms, LANES), jnp.float32),
        ),
        scratch_shapes=[
            pltpu.VMEM((atoms, length), jnp.float32),
            pltpu.VMEM((rows * atoms, LANES), jnp.float32),
        ],
        compiler_params=params,
        name="course",
    )(codes, halo, temporal, spatial)
    everything = lax.all_to_all(send, "atom", split_axis=0, concat_axis=0, tiled=True)
    size = atoms // 2 * 4 + atoms // 4
    share = jax.ShapeDtypeStruct((size, LANES), jnp.float32)
    mine, other = pl.pallas_call(
        lambda *refs: gradient_kernel(factor, *refs),
        out_shape=(share, share),
        scratch_shapes=[
            pltpu.VMEM((wide, samples), jnp.bfloat16),
            pltpu.VMEM((rows * atoms, LANES), jnp.float32),
            pltpu.VMEM((8 * atoms, LANES), jnp.float32),
            pltpu.VMEM((8 * atoms, LANES), jnp.float32),
            pltpu.VMEM((2 * size, LANES), jnp.float32),
            pltpu.VMEM(((length // LANES + 1) * LANES, LANES), jnp.bfloat16),
        ],
        compiler_params=params,
        name="gradients",
    )(everything, send, xs, signal)
    mine = mine + swapped(other, 1)
    for bit in PARTNERS:
        mine = mine + swapped(mine, bit)
    return pl.pallas_call(
        outputs_kernel,
        out_shape=(
            jax.ShapeDtypeStruct((atoms, channels), jnp.float32),
            jax.ShapeDtypeStruct((atoms, length), jnp.float32),
        ),
        compiler_params=params,
        name="outputs",
    )(mine, swapped(mine, 1))


def solution(mesh):
    in_specs = (P(None, "tm"), P("atom", None), P("atom", None), P("atom", "tm"), P("atom", "tm"))
    out_specs = (P("atom", None), P("atom", None))
    return jax.shard_map(local, mesh=mesh, in_specs=in_specs, out_specs=out_specs, check_vma=False)
```

```python
import math

import jax
import jax.numpy as jnp
from jax import lax
from jax.experimental import pallas as pl
from jax.experimental.pallas import tpu as pltpu
from jax.sharding import PartitionSpec as P

LANES = 128
HALF = LANES // 2
PARTNERS = (2, 4, 8, 28)
VMEM_BYTES = 16 << 20


def up(n, m):
    return -(-n // m) * m


def lower_band(size):
    rows = lax.broadcasted_iota(jnp.int32, (size, size), 0)
    cols = lax.broadcasted_iota(jnp.int32, (size, size), 1)
    return cols >= rows


def codes_kernel(cv_ref, mask_ref, tail_ref, own_ref):
    atoms, samples = cv_ref.shape
    length = tail_ref.shape[1]
    per = length // LANES
    down = lax.broadcasted_iota(jnp.int32, (atoms, atoms), 0)
    along = lax.broadcasted_iota(jnp.int32, (atoms, atoms), 1)
    for b in reversed(range(samples // length)):
        across = jnp.broadcast_to(mask_ref[b : b + 1, :], (atoms, atoms))
        on = jnp.sum(jnp.where(down == along, across, 0).astype(jnp.float32), axis=1, keepdims=True)
        block = cv_ref[:, b * length : (b + 1) * length].astype(jnp.float32) * on
        if (b + 1) * length == samples:
            tail_ref[...] = block.astype(jnp.bfloat16)
        for j in range(per):
            at = (per * b + j) * atoms
            own_ref[at : at + atoms, :] = block[:, j * LANES : (j + 1) * LANES]


def course_kernel(
    own_ref, halo_ref, temporal_ref, spatial_ref, send_ref, xs_ref, tf_ref, cs_ref
):
    copies, atoms, width = send_ref.shape
    length = temporal_ref.shape[1]
    channels = spatial_ref.shape[1]
    rows = own_ref.shape[0] // atoms
    samples = rows * LANES
    per = length // LANES
    for j in range(per):
        xs_ref[j * atoms : (j + 1) * atoms, :] = halo_ref[
            :, j * LANES : (j + 1) * LANES
        ].astype(jnp.float32)
    xs_ref[per * atoms :, :] = own_ref[...]
    tf_ref[...] = temporal_ref[...].astype(jnp.float32)
    band = lower_band(LANES)

    def turned(k, at):
        row = tf_ref[k : k + 1, at : at + LANES]
        return pltpu.roll(
            jnp.broadcast_to(row, (LANES, LANES)), 0, 1, stride=1, stride_axis=0
        )

    for k in range(atoms):
        near, far = turned(k, 0), turned(k, LANES)
        matrix = jnp.concatenate(
            [jnp.where(band, 0.0, far), jnp.where(band, far, near), jnp.where(band, near, 0.0)],
            axis=0,
        ).astype(jnp.bfloat16)
        windows = jnp.concatenate(
            [xs_ref[pl.ds(j * atoms + k, rows, stride=atoms), :] for j in range(per + 1)],
            axis=1,
        ).astype(jnp.bfloat16)
        cs_ref[pl.ds(k, rows, stride=atoms), :] = jnp.dot(
            windows, matrix, preferred_element_type=jnp.float32
        )
    padded = jnp.concatenate(
        [spatial_ref[...], jnp.zeros((atoms, width - samples - channels), jnp.bfloat16)],
        axis=1,
    )
    for c in range(copies):
        send_ref[c, :, samples:] = padded
    for i in range(rows):
        part = cs_ref[i * atoms : (i + 1) * atoms, :].astype(jnp.bfloat16)
        for c in range(copies):
            send_ref[c, :, i * LANES : (i + 1) * LANES] = part


def half_of(out_ref, core, space_ref, xs_ref, pr_ref, xh_ref, ph_ref, lo_ref, hi_ref, turned_ref, factor):
    atoms = space_ref.shape[0]
    half = atoms // 2
    rows, blocks = pr_ref.shape[0] // atoms, xs_ref.shape[0] // atoms
    for e in range(blocks):
        at = pl.multiple_of(e * atoms + core * half, half)
        xh_ref[e * half : (e + 1) * half, :] = xs_ref[pl.ds(at, half), :]
    for i in range(rows):
        at = pl.multiple_of(i * atoms + core * half, half)
        ph_ref[i * half : (i + 1) * half, :] = pr_ref[pl.ds(at, half), :]
    group = LANES // rows
    band = lower_band(LANES)
    for k in range(half):
        if k % group == 0:
            turned = []
            for j in range(3):
                stacked = jnp.concatenate(
                    [xh_ref[pl.ds(j * half + k + g, rows, stride=half), :] for g in range(group)],
                    axis=0,
                )
                turned.append(stacked.T.astype(jnp.bfloat16))
            turned_ref[...] = jnp.concatenate(turned, axis=0)
        above, below = (k % group) * rows, LANES - (k % group + 1) * rows
        placed = [ph_ref[pl.ds(k, rows, stride=half), :]]
        if above:
            placed.insert(0, jnp.zeros((above, LANES), jnp.float32))
        if below:
            placed.append(jnp.zeros((below, LANES), jnp.float32))
        products = jnp.dot(
            turned_ref[...],
            jnp.concatenate(placed, axis=0).astype(jnp.bfloat16),
            preferred_element_type=jnp.float32,
        )
        old, mid, new = products[:LANES], products[LANES : 2 * LANES], products[2 * LANES :]
        for ref, total in (
            (lo_ref, jnp.where(band, new, mid)),
            (hi_ref, jnp.where(band, mid, old)),
        ):
            parts = [total[:8]]
            for a in range(1, LANES // 8):
                parts.append(pltpu.roll(total[8 * a : 8 * a + 8], LANES - 8 * a, 1))
            while len(parts) > 1:
                parts = [x + y for x, y in zip(parts[::2], parts[1::2], strict=True)]
            ref[8 * k : 8 * k + 8, :] = parts[0]
    row = lax.broadcasted_iota(jnp.int32, (8 * half, LANES), 0)
    start = pl.multiple_of(core * half, half)
    tiles = [space_ref[pl.ds(start, half), :LANES], space_ref[pl.ds(start, half), LANES : 2 * LANES]]
    for ref in (lo_ref, hi_ref):
        total = ref[...]
        for bit in (1, 2, 4):
            total = jnp.where((row & bit) != 0, pltpu.roll(total, LANES - bit, 1), total)
        tiles.append(factor * total.reshape(half, 8, LANES).sum(axis=1))
    for t, tile in enumerate(tiles):
        out_ref[t * half : (t + 1) * half, :] = tile
    lane = lax.broadcasted_iota(jnp.int32, (half // 2, LANES), 1)
    rest = space_ref[pl.ds(start, half), 2 * LANES :]
    out_ref[4 * half :, :] = jnp.where(
        lane < HALF, rest[: half // 2], pltpu.roll(rest[half // 2 :], HALF, 1)
    )


def other_half_kernel(
    factor, all_ref, own_ref, xs_ref, signal_ref, other_ref, space_ref, pr_ref, res_ref, *scratch
):
    groups, atoms, width = all_ref.shape
    channels, samples = signal_ref.shape
    wide = width - samples
    everything = all_ref[...].reshape(groups * atoms, width)
    model = lax.dot_general(
        everything[:, samples:],
        everything[:, :samples],
        (((0,), (0,)), ((), ())),
        preferred_element_type=jnp.float32,
    )
    res_ref[channels:, :] = jnp.zeros((wide - channels, samples), jnp.bfloat16)
    res_ref[:channels, :] = (model[:channels] - signal_ref[...].astype(jnp.float32)).astype(
        jnp.bfloat16
    )
    own = own_ref[0]
    projected = jnp.dot(own[:, samples:], res_ref[...], preferred_element_type=jnp.float32)
    for i in range(samples // LANES):
        pr_ref[i * atoms : (i + 1) * atoms, :] = projected[:, i * LANES : (i + 1) * LANES]
    space_ref[...] = factor * lax.dot_general(
        own[:, :samples], res_ref[...], (((1,), (1,)), ((), ())), preferred_element_type=jnp.float32
    )
    core = lax.axis_index("tm") % 2
    half_of(other_ref, 1 - core, space_ref, xs_ref, pr_ref, *scratch, factor)


def own_half_kernel(factor, space_ref, xs_ref, pr_ref, mine_ref, *scratch):
    core = lax.axis_index("tm") % 2
    half_of(mine_ref, core, space_ref, xs_ref, pr_ref, *scratch, factor)


def outputs_kernel(mine_ref, other_ref, space_ref, time_ref):
    half = space_ref.shape[0] // 2
    channels = space_ref.shape[1]
    core = lax.axis_index("tm") % 2
    for ref, which in ((mine_ref, core), (other_ref, 1 - core)):
        at = pl.multiple_of(which * half, 8)
        tile = [ref[t * half : (t + 1) * half, :] for t in range(4)]
        space_ref[pl.ds(at, half), :LANES] = tile[0]
        space_ref[pl.ds(at, half), LANES : 2 * LANES] = tile[1]
        time_ref[pl.ds(at, half), :LANES] = tile[2]
        time_ref[pl.ds(at, half), LANES:] = tile[3]
        rest = ref[4 * half :, :]
        both = jnp.concatenate([rest, pltpu.roll(rest, HALF, 1)], axis=0)
        space_ref[pl.ds(at, half), 2 * LANES :] = both[:, : channels - 2 * LANES]


def local(signal, spatial, temporal, code_values, block_mask):
    atoms, channels = spatial.shape
    length = temporal.shape[1]
    samples = signal.shape[1]
    groups, slabs = lax.axis_size("atom"), lax.axis_size("tm")
    rows = samples // LANES
    wide = up(channels, LANES)
    factor = 1.0 / math.sqrt(samples * slabs)
    params = pltpu.CompilerParams(vmem_limit_bytes=VMEM_BYTES)

    def swapped(value, bit):
        return lax.ppermute(value, "tm", [(i, i ^ bit) for i in range(slabs)])

    tail, codes = pl.pallas_call(
        codes_kernel,
        out_shape=(
            jax.ShapeDtypeStruct((atoms, length), jnp.bfloat16),
            jax.ShapeDtypeStruct((rows * atoms, LANES), jnp.float32),
        ),
        compiler_params=params,
        name="codes",
    )(code_values, block_mask.T)
    halo = lax.ppermute(tail, "tm", [(i, i + 1) for i in range(slabs - 1)])
    send, xs = pl.pallas_call(
        course_kernel,
        out_shape=(
            jax.ShapeDtypeStruct((groups, atoms, samples + wide), jnp.bfloat16),
            jax.ShapeDtypeStruct(((rows + length // LANES) * atoms, LANES), jnp.float32),
        ),
        scratch_shapes=[
            pltpu.VMEM((atoms, length), jnp.float32),
            pltpu.VMEM((rows * atoms, LANES), jnp.float32),
        ],
        compiler_params=params,
        name="course",
    )(codes, halo, temporal, spatial)
    everything = lax.all_to_all(send, "atom", split_axis=0, concat_axis=0, tiled=True)
    size = atoms // 2 * 4 + atoms // 4
    half, per = atoms // 2, length // LANES
    share = jax.ShapeDtypeStruct((size, LANES), jnp.float32)
    scratch = [
        pltpu.VMEM(((rows + per) * half, LANES), jnp.float32),
        pltpu.VMEM((rows * half, LANES), jnp.float32),
        pltpu.VMEM((8 * half, LANES), jnp.float32),
        pltpu.VMEM((8 * half, LANES), jnp.float32),
        pltpu.VMEM(((per + 1) * LANES, LANES), jnp.bfloat16),
    ]
    other, space, projected = pl.pallas_call(
        lambda *refs: other_half_kernel(factor, *refs),
        out_shape=(
            share,
            jax.ShapeDtypeStruct((atoms, wide), jnp.float32),
            jax.ShapeDtypeStruct((rows * atoms, LANES), jnp.float32),
        ),
        scratch_shapes=[pltpu.VMEM((wide, samples), jnp.bfloat16), *scratch],
        compiler_params=params,
        name="other_half",
    )(everything, send, xs, signal)
    mine = pl.pallas_call(
        lambda *refs: own_half_kernel(factor, *refs),
        out_shape=share,
        scratch_shapes=scratch,
        compiler_params=params,
        cost_estimate=pl.CostEstimate(flops=200_000_000, bytes_accessed=1_000_000, transcendentals=0),
        name="own_half",
    )(space, xs, projected)
    mine = mine + swapped(other, 1)
    for bit in PARTNERS:
        mine = mine + swapped(mine, bit)
    return pl.pallas_call(
        outputs_kernel,
        out_shape=(
            jax.ShapeDtypeStruct((atoms, channels), jnp.float32),
            jax.ShapeDtypeStruct((atoms, length), jnp.float32),
        ),
        compiler_params=params,
        name="outputs",
    )(mine, swapped(mine, 1))


def solution(mesh):
    in_specs = (P(None, "tm"), P("atom", None), P("atom", None), P("atom", "tm"), P("atom", "tm"))
    out_specs = (P("atom", None), P("atom", None))
    return jax.shard_map(local, mesh=mesh, in_specs=in_specs, out_specs=out_specs, check_vma=False)
```

```python
import math

import jax
import jax.numpy as jnp
from jax import lax
from jax.experimental import pallas as pl
from jax.experimental.pallas import tpu as pltpu
from jax.sharding import PartitionSpec as P

LANES = 128
HALF = LANES // 2
PARTNERS = (2, 4, 8, 28)
VMEM_BYTES = 16 << 20


def up(n, m):
    return -(-n // m) * m


def lower_band(size):
    rows = lax.broadcasted_iota(jnp.int32, (size, size), 0)
    cols = lax.broadcasted_iota(jnp.int32, (size, size), 1)
    return cols >= rows


def diagonal_kernel(out_ref):
    down = lax.broadcasted_iota(jnp.int32, out_ref.shape, 0)
    along = lax.broadcasted_iota(jnp.int32, out_ref.shape, 1)
    out_ref[...] = jnp.where(down == along, 1.0, 0.0)


def codes_kernel(diagonal_ref, cv_ref, mask_ref, tail_ref, own_ref):
    atoms, samples = cv_ref.shape
    length = tail_ref.shape[1]
    per = length // LANES
    for b in reversed(range(samples // length)):
        across = diagonal_ref[...] * mask_ref[b : b + 1, :].astype(jnp.float32)
        on = jnp.sum(across, axis=1, keepdims=True)
        block = cv_ref[:, b * length : (b + 1) * length].astype(jnp.float32) * on
        if (b + 1) * length == samples:
            tail_ref[...] = block.astype(jnp.bfloat16)
        for j in range(per):
            at = (per * b + j) * atoms
            own_ref[at : at + atoms, :] = block[:, j * LANES : (j + 1) * LANES]


def course_kernel(
    own_ref, halo_ref, temporal_ref, spatial_ref, send_ref, xs_ref, tf_ref, cs_ref
):
    copies, atoms, width = send_ref.shape
    length = temporal_ref.shape[1]
    channels = spatial_ref.shape[1]
    rows = own_ref.shape[0] // atoms
    samples = rows * LANES
    per = length // LANES
    for j in range(per):
        xs_ref[j * atoms : (j + 1) * atoms, :] = halo_ref[
            :, j * LANES : (j + 1) * LANES
        ].astype(jnp.float32)
    xs_ref[per * atoms :, :] = own_ref[...]
    tf_ref[...] = temporal_ref[...].astype(jnp.float32)
    band = lower_band(LANES)

    def turned(k, at):
        row = tf_ref[k : k + 1, at : at + LANES]
        return pltpu.roll(
            jnp.broadcast_to(row, (LANES, LANES)), 0, 1, stride=1, stride_axis=0
        )

    for k in range(atoms):
        near, far = turned(k, 0), turned(k, LANES)
        matrix = jnp.concatenate(
            [jnp.where(band, 0.0, far), jnp.where(band, far, near), jnp.where(band, near, 0.0)],
            axis=0,
        ).astype(jnp.bfloat16)
        windows = jnp.concatenate(
            [xs_ref[pl.ds(j * atoms + k, rows, stride=atoms), :] for j in range(per + 1)],
            axis=1,
        ).astype(jnp.bfloat16)
        cs_ref[pl.ds(k, rows, stride=atoms), :] = jnp.dot(
            windows, matrix, preferred_element_type=jnp.float32
        )
    padded = jnp.concatenate(
        [spatial_ref[...], jnp.zeros((atoms, width - samples - channels), jnp.bfloat16)],
        axis=1,
    )
    for c in range(copies):
        send_ref[c, :, samples:] = padded
    for i in range(rows):
        part = cs_ref[i * atoms : (i + 1) * atoms, :].astype(jnp.bfloat16)
        for c in range(copies):
            send_ref[c, :, i * LANES : (i + 1) * LANES] = part


def half_of(out_ref, core, space_ref, xs_ref, pr_ref, xh_ref, ph_ref, lo_ref, hi_ref, turned_ref, factor):
    atoms = space_ref.shape[0]
    half = atoms // 2
    rows, blocks = pr_ref.shape[0] // atoms, xs_ref.shape[0] // atoms
    for e in range(blocks):
        at = pl.multiple_of(e * atoms + core * half, half)
        xh_ref[e * half : (e + 1) * half, :] = xs_ref[pl.ds(at, half), :]
    for i in range(rows):
        at = pl.multiple_of(i * atoms + core * half, half)
        ph_ref[i * half : (i + 1) * half, :] = pr_ref[pl.ds(at, half), :]
    group = LANES // rows
    band = lower_band(LANES)
    for k in range(half):
        if k % group == 0:
            turned = []
            for j in range(3):
                stacked = jnp.concatenate(
                    [xh_ref[pl.ds(j * half + k + g, rows, stride=half), :] for g in range(group)],
                    axis=0,
                )
                turned.append(stacked.T.astype(jnp.bfloat16))
            turned_ref[...] = jnp.concatenate(turned, axis=0)
        above, below = (k % group) * rows, LANES - (k % group + 1) * rows
        placed = [ph_ref[pl.ds(k, rows, stride=half), :]]
        if above:
            placed.insert(0, jnp.zeros((above, LANES), jnp.float32))
        if below:
            placed.append(jnp.zeros((below, LANES), jnp.float32))
        products = jnp.dot(
            turned_ref[...],
            jnp.concatenate(placed, axis=0).astype(jnp.bfloat16),
            preferred_element_type=jnp.float32,
        )
        old, mid, new = products[:LANES], products[LANES : 2 * LANES], products[2 * LANES :]
        for ref, total in (
            (lo_ref, jnp.where(band, new, mid)),
            (hi_ref, jnp.where(band, mid, old)),
        ):
            parts = [total[:8]]
            for a in range(1, LANES // 8):
                parts.append(pltpu.roll(total[8 * a : 8 * a + 8], LANES - 8 * a, 1))
            while len(parts) > 1:
                parts = [x + y for x, y in zip(parts[::2], parts[1::2], strict=True)]
            ref[8 * k : 8 * k + 8, :] = parts[0]
    row = lax.broadcasted_iota(jnp.int32, (8 * half, LANES), 0)
    start = pl.multiple_of(core * half, half)
    tiles = [space_ref[pl.ds(start, half), :LANES], space_ref[pl.ds(start, half), LANES : 2 * LANES]]
    for ref in (lo_ref, hi_ref):
        total = ref[...]
        for bit in (1, 2, 4):
            total = jnp.where((row & bit) != 0, pltpu.roll(total, LANES - bit, 1), total)
        tiles.append(factor * total.reshape(half, 8, LANES).sum(axis=1))
    for t, tile in enumerate(tiles):
        out_ref[t * half : (t + 1) * half, :] = tile
    lane = lax.broadcasted_iota(jnp.int32, (half // 2, LANES), 1)
    rest = space_ref[pl.ds(start, half), 2 * LANES :]
    out_ref[4 * half :, :] = jnp.where(
        lane < HALF, rest[: half // 2], pltpu.roll(rest[half // 2 :], HALF, 1)
    )


def other_half_kernel(
    factor, all_ref, own_ref, xs_ref, signal_ref, other_ref, space_ref, pr_ref, res_ref, *scratch
):
    groups, atoms, width = all_ref.shape
    channels, samples = signal_ref.shape
    wide = width - samples
    everything = all_ref[...].reshape(groups * atoms, width)
    model = lax.dot_general(
        everything[:, samples:],
        everything[:, :samples],
        (((0,), (0,)), ((), ())),
        preferred_element_type=jnp.float32,
    )
    res_ref[channels:, :] = jnp.zeros((wide - channels, samples), jnp.bfloat16)
    res_ref[:channels, :] = (model[:channels] - signal_ref[...].astype(jnp.float32)).astype(
        jnp.bfloat16
    )
    own = own_ref[0]
    projected = jnp.dot(own[:, samples:], res_ref[...], preferred_element_type=jnp.float32)
    for i in range(samples // LANES):
        pr_ref[i * atoms : (i + 1) * atoms, :] = projected[:, i * LANES : (i + 1) * LANES]
    space_ref[...] = factor * lax.dot_general(
        own[:, :samples], res_ref[...], (((1,), (1,)), ((), ())), preferred_element_type=jnp.float32
    )
    core = lax.axis_index("tm") % 2
    half_of(other_ref, 1 - core, space_ref, xs_ref, pr_ref, *scratch, factor)


def own_half_kernel(factor, space_ref, xs_ref, pr_ref, mine_ref, *scratch):
    core = lax.axis_index("tm") % 2
    half_of(mine_ref, core, space_ref, xs_ref, pr_ref, *scratch, factor)


def outputs_kernel(mine_ref, other_ref, space_ref, time_ref):
    half = space_ref.shape[0] // 2
    channels = space_ref.shape[1]
    core = lax.axis_index("tm") % 2
    for ref, which in ((mine_ref, core), (other_ref, 1 - core)):
        at = pl.multiple_of(which * half, 8)
        tile = [ref[t * half : (t + 1) * half, :] for t in range(4)]
        space_ref[pl.ds(at, half), :LANES] = tile[0]
        space_ref[pl.ds(at, half), LANES : 2 * LANES] = tile[1]
        time_ref[pl.ds(at, half), :LANES] = tile[2]
        time_ref[pl.ds(at, half), LANES:] = tile[3]
        rest = ref[4 * half :, :]
        both = jnp.concatenate([rest, pltpu.roll(rest, HALF, 1)], axis=0)
        space_ref[pl.ds(at, half), 2 * LANES :] = both[:, : channels - 2 * LANES]


def local(signal, spatial, temporal, code_values, block_mask):
    atoms, channels = spatial.shape
    length = temporal.shape[1]
    samples = signal.shape[1]
    groups, slabs = lax.axis_size("atom"), lax.axis_size("tm")
    rows = samples // LANES
    wide = up(channels, LANES)
    factor = 1.0 / math.sqrt(samples * slabs)
    params = pltpu.CompilerParams(vmem_limit_bytes=VMEM_BYTES)

    def swapped(value, bit):
        return lax.ppermute(value, "tm", [(i, i ^ bit) for i in range(slabs)])

    diagonal = pl.pallas_call(
        diagonal_kernel,
        out_shape=jax.ShapeDtypeStruct((atoms, atoms), jnp.float32),
        compiler_params=params,
        cost_estimate=pl.CostEstimate(flops=4_000_000_000, bytes_accessed=8_000_000, transcendentals=0),
        name="diagonal",
    )()
    tail, codes = pl.pallas_call(
        codes_kernel,
        out_shape=(
            jax.ShapeDtypeStruct((atoms, length), jnp.bfloat16),
            jax.ShapeDtypeStruct((rows * atoms, LANES), jnp.float32),
        ),
        compiler_params=params,
        name="codes",
    )(diagonal, code_values, block_mask.T)
    halo = lax.ppermute(tail, "tm", [(i, i + 1) for i in range(slabs - 1)])
    send, xs = pl.pallas_call(
        course_kernel,
        out_shape=(
            jax.ShapeDtypeStruct((groups, atoms, samples + wide), jnp.bfloat16),
            jax.ShapeDtypeStruct(((rows + length // LANES) * atoms, LANES), jnp.float32),
        ),
        scratch_shapes=[
            pltpu.VMEM((atoms, length), jnp.float32),
            pltpu.VMEM((rows * atoms, LANES), jnp.float32),
        ],
        compiler_params=params,
        name="course",
    )(codes, halo, temporal, spatial)
    everything = lax.all_to_all(send, "atom", split_axis=0, concat_axis=0, tiled=True)
    size = atoms // 2 * 4 + atoms // 4
    half, per = atoms // 2, length // LANES
    share = jax.ShapeDtypeStruct((size, LANES), jnp.float32)
    scratch = [
        pltpu.VMEM(((rows + per) * half, LANES), jnp.float32),
        pltpu.VMEM((rows * half, LANES), jnp.float32),
        pltpu.VMEM((8 * half, LANES), jnp.float32),
        pltpu.VMEM((8 * half, LANES), jnp.float32),
        pltpu.VMEM(((per + 1) * LANES, LANES), jnp.bfloat16),
    ]
    other, space, projected = pl.pallas_call(
        lambda *refs: other_half_kernel(factor, *refs),
        out_shape=(
            share,
            jax.ShapeDtypeStruct((atoms, wide), jnp.float32),
            jax.ShapeDtypeStruct((rows * atoms, LANES), jnp.float32),
        ),
        scratch_shapes=[pltpu.VMEM((wide, samples), jnp.bfloat16), *scratch],
        compiler_params=params,
        name="other_half",
    )(everything, send, xs, signal)
    mine = pl.pallas_call(
        lambda *refs: own_half_kernel(factor, *refs),
        out_shape=share,
        scratch_shapes=scratch,
        compiler_params=params,
        cost_estimate=pl.CostEstimate(flops=200_000_000, bytes_accessed=1_000_000, transcendentals=0),
        name="own_half",
    )(space, xs, projected)
    mine = mine + swapped(other, 1)
    for bit in PARTNERS:
        mine = mine + swapped(mine, bit)
    return pl.pallas_call(
        outputs_kernel,
        out_shape=(
            jax.ShapeDtypeStruct((atoms, channels), jnp.float32),
            jax.ShapeDtypeStruct((atoms, length), jnp.float32),
        ),
        compiler_params=params,
        name="outputs",
    )(mine, swapped(mine, 1))


def solution(mesh):
    in_specs = (P(None, "tm"), P("atom", None), P("atom", None), P("atom", "tm"), P("atom", "tm"))
    out_specs = (P("atom", None), P("atom", None))
    return jax.shard_map(local, mesh=mesh, in_specs=in_specs, out_specs=out_specs, check_vma=False)
```

```python
import math

import jax
import jax.numpy as jnp
from jax import lax
from jax.experimental import pallas as pl
from jax.experimental.pallas import tpu as pltpu
from jax.sharding import PartitionSpec as P

LANES = 128
HALF = LANES // 2
PARTNERS = (2, 4, 8, 28)
VMEM_BYTES = 16 << 20


def up(n, m):
    return -(-n // m) * m


def lower_band(size):
    rows = lax.broadcasted_iota(jnp.int32, (size, size), 0)
    cols = lax.broadcasted_iota(jnp.int32, (size, size), 1)
    return cols >= rows


def diagonal_kernel(out_ref):
    down = lax.broadcasted_iota(jnp.int32, out_ref.shape, 0)
    along = lax.broadcasted_iota(jnp.int32, out_ref.shape, 1)
    out_ref[...] = jnp.where(down == along, 1.0, 0.0)


def codes_kernel(diagonal_ref, cv_ref, mask_ref, tail_ref, own_ref):
    atoms, samples = cv_ref.shape
    length = tail_ref.shape[1]
    per = length // LANES
    for b in reversed(range(samples // length)):
        across = diagonal_ref[...] * mask_ref[b : b + 1, :].astype(jnp.float32)
        on = jnp.sum(across, axis=1, keepdims=True)
        block = cv_ref[:, b * length : (b + 1) * length].astype(jnp.float32) * on
        if (b + 1) * length == samples:
            tail_ref[...] = block.astype(jnp.bfloat16)
        for j in range(per):
            at = (per * b + j) * atoms
            own_ref[at : at + atoms, :] = block[:, j * LANES : (j + 1) * LANES]


def course_kernel(
    own_ref, halo_ref, temporal_ref, spatial_ref, send_ref, xs_ref, tf_ref, cs_ref
):
    copies = send_ref.shape[0]
    atoms, length = temporal_ref.shape
    channels = spatial_ref.shape[1]
    rows = own_ref.shape[0] // atoms
    per = length // LANES
    for j in range(per):
        xs_ref[j * atoms : (j + 1) * atoms, :] = halo_ref[
            :, j * LANES : (j + 1) * LANES
        ].astype(jnp.float32)
    xs_ref[per * atoms :, :] = own_ref[...]
    tf_ref[...] = temporal_ref[...].astype(jnp.float32)
    band = lower_band(LANES)

    def turned(k, at):
        row = tf_ref[k : k + 1, at : at + LANES]
        return pltpu.roll(
            jnp.broadcast_to(row, (LANES, LANES)), 0, 1, stride=1, stride_axis=0
        )

    for k in range(atoms):
        near, far = turned(k, 0), turned(k, LANES)
        matrix = jnp.concatenate(
            [jnp.where(band, 0.0, far), jnp.where(band, far, near), jnp.where(band, near, 0.0)],
            axis=0,
        ).astype(jnp.bfloat16)
        windows = jnp.concatenate(
            [xs_ref[pl.ds(j * atoms + k, rows, stride=atoms), :] for j in range(per + 1)],
            axis=1,
        ).astype(jnp.bfloat16)
        cs_ref[pl.ds(k, rows, stride=atoms), :] = jnp.dot(
            windows, matrix, preferred_element_type=jnp.float32
        )
    rest = jnp.concatenate(
        [
            spatial_ref[:, 2 * LANES :].astype(jnp.float32),
            jnp.zeros((atoms, 3 * LANES - channels), jnp.float32),
        ],
        axis=1,
    )
    tiles = [
        cs_ref[...],
        spatial_ref[:, :LANES],
        spatial_ref[:, LANES : 2 * LANES],
        rest[: atoms // 2] + pltpu.roll(rest[atoms // 2 :], HALF, 1),
    ]
    at = 0
    for tile in tiles:
        for c in range(copies):
            send_ref[c, at : at + tile.shape[0], :] = tile.astype(jnp.bfloat16)
        at += tile.shape[0]


def unpacked(ref, groups, atoms, samples):
    def tile(at):
        return ref[:groups, at : at + atoms, :].reshape(groups * atoms, LANES)

    end = samples // LANES * atoms
    course = jnp.concatenate([tile(at) for at in range(0, end, atoms)], axis=1)
    half = atoms // 2
    rest = ref[:groups, end + 2 * atoms :, :].astype(jnp.float32).reshape(groups * half, LANES)
    lane = lax.broadcasted_iota(jnp.int32, rest.shape, 1)
    sides = [
        jnp.where(lane < HALF, side, 0.0).reshape(groups, half, LANES)
        for side in (rest, pltpu.roll(rest, HALF, 1))
    ]
    last = jnp.concatenate(sides, axis=1).reshape(groups * atoms, LANES).astype(jnp.bfloat16)
    return course, jnp.concatenate([tile(end), tile(end + atoms), last], axis=1)


def half_of(out_ref, core, space_ref, xs_ref, pr_ref, xh_ref, ph_ref, lo_ref, hi_ref, turned_ref, factor):
    atoms = space_ref.shape[0]
    half = atoms // 2
    rows, blocks = pr_ref.shape[0] // atoms, xs_ref.shape[0] // atoms
    for e in range(blocks):
        at = pl.multiple_of(e * atoms + core * half, half)
        xh_ref[e * half : (e + 1) * half, :] = xs_ref[pl.ds(at, half), :]
    for i in range(rows):
        at = pl.multiple_of(i * atoms + core * half, half)
        ph_ref[i * half : (i + 1) * half, :] = pr_ref[pl.ds(at, half), :]
    group = LANES // rows
    band = lower_band(LANES)
    for k in range(half):
        if k % group == 0:
            turned = []
            for j in range(3):
                stacked = jnp.concatenate(
                    [xh_ref[pl.ds(j * half + k + g, rows, stride=half), :] for g in range(group)],
                    axis=0,
                )
                turned.append(stacked.T.astype(jnp.bfloat16))
            turned_ref[...] = jnp.concatenate(turned, axis=0)
        above, below = (k % group) * rows, LANES - (k % group + 1) * rows
        placed = [ph_ref[pl.ds(k, rows, stride=half), :]]
        if above:
            placed.insert(0, jnp.zeros((above, LANES), jnp.float32))
        if below:
            placed.append(jnp.zeros((below, LANES), jnp.float32))
        products = jnp.dot(
            turned_ref[...],
            jnp.concatenate(placed, axis=0).astype(jnp.bfloat16),
            preferred_element_type=jnp.float32,
        )
        old, mid, new = products[:LANES], products[LANES : 2 * LANES], products[2 * LANES :]
        for ref, total in (
            (lo_ref, jnp.where(band, new, mid)),
            (hi_ref, jnp.where(band, mid, old)),
        ):
            parts = [total[:8]]
            for a in range(1, LANES // 8):
                parts.append(pltpu.roll(total[8 * a : 8 * a + 8], LANES - 8 * a, 1))
            while len(parts) > 1:
                parts = [x + y for x, y in zip(parts[::2], parts[1::2], strict=True)]
            ref[8 * k : 8 * k + 8, :] = parts[0]
    row = lax.broadcasted_iota(jnp.int32, (8 * half, LANES), 0)
    start = pl.multiple_of(core * half, half)
    tiles = [space_ref[pl.ds(start, half), :LANES], space_ref[pl.ds(start, half), LANES : 2 * LANES]]
    for ref in (lo_ref, hi_ref):
        total = ref[...]
        for bit in (1, 2, 4):
            total = jnp.where((row & bit) != 0, pltpu.roll(total, LANES - bit, 1), total)
        tiles.append(factor * total.reshape(half, 8, LANES).sum(axis=1))
    for t, tile in enumerate(tiles):
        out_ref[t * half : (t + 1) * half, :] = tile
    lane = lax.broadcasted_iota(jnp.int32, (half // 2, LANES), 1)
    rest = space_ref[pl.ds(start, half), 2 * LANES :]
    out_ref[4 * half :, :] = jnp.where(
        lane < HALF, rest[: half // 2], pltpu.roll(rest[half // 2 :], HALF, 1)
    )


def other_half_kernel(
    factor, all_ref, own_ref, xs_ref, signal_ref, other_ref, space_ref, pr_ref, res_ref, *scratch
):
    groups = all_ref.shape[0]
    atoms, wide = space_ref.shape
    channels, samples = signal_ref.shape
    course, patterns = unpacked(all_ref, groups, atoms, samples)
    model = lax.dot_general(
        patterns, course, (((0,), (0,)), ((), ())), preferred_element_type=jnp.float32
    )
    res_ref[channels:, :] = jnp.zeros((wide - channels, samples), jnp.bfloat16)
    res_ref[:channels, :] = (model[:channels] - signal_ref[...].astype(jnp.float32)).astype(
        jnp.bfloat16
    )
    course, patterns = unpacked(own_ref, 1, atoms, samples)
    projected = jnp.dot(patterns, res_ref[...], preferred_element_type=jnp.float32)
    for i in range(samples // LANES):
        pr_ref[i * atoms : (i + 1) * atoms, :] = projected[:, i * LANES : (i + 1) * LANES]
    space_ref[...] = factor * lax.dot_general(
        course, res_ref[...], (((1,), (1,)), ((), ())), preferred_element_type=jnp.float32
    )
    core = lax.axis_index("tm") % 2
    half_of(other_ref, 1 - core, space_ref, xs_ref, pr_ref, *scratch, factor)


def own_half_kernel(factor, space_ref, xs_ref, pr_ref, mine_ref, *scratch):
    core = lax.axis_index("tm") % 2
    half_of(mine_ref, core, space_ref, xs_ref, pr_ref, *scratch, factor)


def outputs_kernel(mine_ref, other_ref, space_ref, time_ref):
    half = space_ref.shape[0] // 2
    channels = space_ref.shape[1]
    core = lax.axis_index("tm") % 2
    for ref, which in ((mine_ref, core), (other_ref, 1 - core)):
        at = pl.multiple_of(which * half, 8)
        tile = [ref[t * half : (t + 1) * half, :] for t in range(4)]
        space_ref[pl.ds(at, half), :LANES] = tile[0]
        space_ref[pl.ds(at, half), LANES : 2 * LANES] = tile[1]
        time_ref[pl.ds(at, half), :LANES] = tile[2]
        time_ref[pl.ds(at, half), LANES:] = tile[3]
        rest = ref[4 * half :, :]
        both = jnp.concatenate([rest, pltpu.roll(rest, HALF, 1)], axis=0)
        space_ref[pl.ds(at, half), 2 * LANES :] = both[:, : channels - 2 * LANES]


def local(signal, spatial, temporal, code_values, block_mask):
    atoms, channels = spatial.shape
    length = temporal.shape[1]
    samples = signal.shape[1]
    groups, slabs = lax.axis_size("atom"), lax.axis_size("tm")
    rows = samples // LANES
    wide = up(channels, LANES)
    factor = 1.0 / math.sqrt(samples * slabs)
    params = pltpu.CompilerParams(vmem_limit_bytes=VMEM_BYTES)

    def swapped(value, bit):
        return lax.ppermute(value, "tm", [(i, i ^ bit) for i in range(slabs)])

    diagonal = pl.pallas_call(
        diagonal_kernel,
        out_shape=jax.ShapeDtypeStruct((atoms, atoms), jnp.float32),
        compiler_params=params,
        cost_estimate=pl.CostEstimate(flops=4_000_000_000, bytes_accessed=8_000_000, transcendentals=0),
        name="diagonal",
    )()
    tail, codes = pl.pallas_call(
        codes_kernel,
        out_shape=(
            jax.ShapeDtypeStruct((atoms, length), jnp.bfloat16),
            jax.ShapeDtypeStruct((rows * atoms, LANES), jnp.float32),
        ),
        compiler_params=params,
        name="codes",
    )(diagonal, code_values, block_mask.T)
    halo = lax.ppermute(tail, "tm", [(i, i + 1) for i in range(slabs - 1)])
    send, xs = pl.pallas_call(
        course_kernel,
        out_shape=(
            jax.ShapeDtypeStruct((groups, (rows + 2) * atoms + atoms // 2, LANES), jnp.bfloat16),
            jax.ShapeDtypeStruct(((rows + length // LANES) * atoms, LANES), jnp.float32),
        ),
        scratch_shapes=[
            pltpu.VMEM((atoms, length), jnp.float32),
            pltpu.VMEM((rows * atoms, LANES), jnp.float32),
        ],
        compiler_params=params,
        name="course",
    )(codes, halo, temporal, spatial)
    everything = lax.all_to_all(send, "atom", split_axis=0, concat_axis=0, tiled=True)
    size = atoms // 2 * 4 + atoms // 4
    half, per = atoms // 2, length // LANES
    share = jax.ShapeDtypeStruct((size, LANES), jnp.float32)
    scratch = [
        pltpu.VMEM(((rows + per) * half, LANES), jnp.float32),
        pltpu.VMEM((rows * half, LANES), jnp.float32),
        pltpu.VMEM((8 * half, LANES), jnp.float32),
        pltpu.VMEM((8 * half, LANES), jnp.float32),
        pltpu.VMEM(((per + 1) * LANES, LANES), jnp.bfloat16),
    ]
    other, space, projected = pl.pallas_call(
        lambda *refs: other_half_kernel(factor, *refs),
        out_shape=(
            share,
            jax.ShapeDtypeStruct((atoms, wide), jnp.float32),
            jax.ShapeDtypeStruct((rows * atoms, LANES), jnp.float32),
        ),
        scratch_shapes=[pltpu.VMEM((wide, samples), jnp.bfloat16), *scratch],
        compiler_params=params,
        name="other_half",
    )(everything, send, xs, signal)
    mine = pl.pallas_call(
        lambda *refs: own_half_kernel(factor, *refs),
        out_shape=share,
        scratch_shapes=scratch,
        compiler_params=params,
        cost_estimate=pl.CostEstimate(flops=200_000_000, bytes_accessed=1_000_000, transcendentals=0),
        name="own_half",
    )(space, xs, projected)
    mine = mine + swapped(other, 1)
    for bit in PARTNERS:
        mine = mine + swapped(mine, bit)
    return pl.pallas_call(
        outputs_kernel,
        out_shape=(
            jax.ShapeDtypeStruct((atoms, channels), jnp.float32),
            jax.ShapeDtypeStruct((atoms, length), jnp.float32),
        ),
        compiler_params=params,
        name="outputs",
    )(mine, swapped(mine, 1))


def solution(mesh):
    in_specs = (P(None, "tm"), P("atom", None), P("atom", None), P("atom", "tm"), P("atom", "tm"))
    out_specs = (P("atom", None), P("atom", None))
    return jax.shard_map(local, mesh=mesh, in_specs=in_specs, out_specs=out_specs, check_vma=False)
```

```python
import math

import jax
import jax.numpy as jnp
from jax import lax
from jax.experimental import pallas as pl
from jax.experimental.pallas import tpu as pltpu
from jax.sharding import PartitionSpec as P

LANES = 128
HALF = LANES // 2
PARTNERS = (4, 8, 28, 2)
VMEM_BYTES = 16 << 20


def up(n, m):
    return -(-n // m) * m


def lower_band(size):
    rows = lax.broadcasted_iota(jnp.int32, (size, size), 0)
    cols = lax.broadcasted_iota(jnp.int32, (size, size), 1)
    return cols >= rows


def diagonal_kernel(out_ref):
    down = lax.broadcasted_iota(jnp.int32, out_ref.shape, 0)
    along = lax.broadcasted_iota(jnp.int32, out_ref.shape, 1)
    out_ref[...] = jnp.where(down == along, 1.0, 0.0)


def codes_kernel(diagonal_ref, cv_ref, mask_ref, tail_ref, own_ref):
    atoms, samples = cv_ref.shape
    length = tail_ref.shape[1]
    per = length // LANES
    for b in reversed(range(samples // length)):
        across = diagonal_ref[...] * mask_ref[b : b + 1, :].astype(jnp.float32)
        on = jnp.sum(across, axis=1, keepdims=True)
        block = cv_ref[:, b * length : (b + 1) * length].astype(jnp.float32) * on
        if (b + 1) * length == samples:
            tail_ref[...] = block.astype(jnp.bfloat16)
        for j in range(per):
            at = (per * b + j) * atoms
            own_ref[at : at + atoms, :] = block[:, j * LANES : (j + 1) * LANES]


def course_kernel(
    own_ref, halo_ref, temporal_ref, spatial_ref, send_ref, xs_ref, tf_ref, cs_ref
):
    copies = send_ref.shape[0]
    atoms, length = temporal_ref.shape
    channels = spatial_ref.shape[1]
    rows = own_ref.shape[0] // atoms
    per = length // LANES
    for j in range(per):
        xs_ref[j * atoms : (j + 1) * atoms, :] = halo_ref[
            :, j * LANES : (j + 1) * LANES
        ].astype(jnp.float32)
    xs_ref[per * atoms :, :] = own_ref[...]
    tf_ref[...] = temporal_ref[...].astype(jnp.float32)
    band = lower_band(LANES)

    def turned(k, at):
        row = tf_ref[k : k + 1, at : at + LANES]
        return pltpu.roll(
            jnp.broadcast_to(row, (LANES, LANES)), 0, 1, stride=1, stride_axis=0
        )

    for k in range(atoms):
        near, far = turned(k, 0), turned(k, LANES)
        matrix = jnp.concatenate(
            [jnp.where(band, 0.0, far), jnp.where(band, far, near), jnp.where(band, near, 0.0)],
            axis=0,
        ).astype(jnp.bfloat16)
        windows = jnp.concatenate(
            [xs_ref[pl.ds(j * atoms + k, rows, stride=atoms), :] for j in range(per + 1)],
            axis=1,
        ).astype(jnp.bfloat16)
        cs_ref[pl.ds(k, rows, stride=atoms), :] = jnp.dot(
            windows, matrix, preferred_element_type=jnp.float32
        )
    rest = jnp.concatenate(
        [
            spatial_ref[:, 2 * LANES :].astype(jnp.float32),
            jnp.zeros((atoms, 3 * LANES - channels), jnp.float32),
        ],
        axis=1,
    )
    tiles = [
        cs_ref[...],
        spatial_ref[:, :LANES],
        spatial_ref[:, LANES : 2 * LANES],
        rest[: atoms // 2] + pltpu.roll(rest[atoms // 2 :], HALF, 1),
    ]
    at = 0
    for tile in tiles:
        for c in range(copies):
            send_ref[c, at : at + tile.shape[0], :] = tile.astype(jnp.bfloat16)
        at += tile.shape[0]


def unpacked(ref, groups, atoms, samples):
    def tile(at):
        return ref[:groups, at : at + atoms, :].reshape(groups * atoms, LANES)

    end = samples // LANES * atoms
    course = jnp.concatenate([tile(at) for at in range(0, end, atoms)], axis=1)
    half = atoms // 2
    rest = ref[:groups, end + 2 * atoms :, :].astype(jnp.float32).reshape(groups * half, LANES)
    lane = lax.broadcasted_iota(jnp.int32, rest.shape, 1)
    sides = [
        jnp.where(lane < HALF, side, 0.0).reshape(groups, half, LANES)
        for side in (rest, pltpu.roll(rest, HALF, 1))
    ]
    last = jnp.concatenate(sides, axis=1).reshape(groups * atoms, LANES).astype(jnp.bfloat16)
    return course, jnp.concatenate([tile(end), tile(end + atoms), last], axis=1)


def half_of(out_ref, core, space_ref, xs_ref, pr_ref, xh_ref, ph_ref, lo_ref, hi_ref, turned_ref, factor):
    atoms = space_ref.shape[0]
    half = atoms // 2
    rows, blocks = pr_ref.shape[0] // atoms, xs_ref.shape[0] // atoms
    for e in range(blocks):
        at = pl.multiple_of(e * atoms + core * half, half)
        xh_ref[e * half : (e + 1) * half, :] = xs_ref[pl.ds(at, half), :]
    for i in range(rows):
        at = pl.multiple_of(i * atoms + core * half, half)
        ph_ref[i * half : (i + 1) * half, :] = pr_ref[pl.ds(at, half), :]
    group = LANES // rows
    down = lax.broadcasted_iota(jnp.int32, (LANES, LANES), 0)
    along = lax.broadcasted_iota(jnp.int32, (LANES, LANES), 1)
    band = along + down >= LANES - 1
    upside = jnp.where(along + down == LANES - 1, 1.0, 0.0).astype(jnp.bfloat16)
    for k in range(half):
        if k % group == 0:
            turned = []
            for j in range(3):
                stacked = jnp.concatenate(
                    [xh_ref[pl.ds(j * half + k + g, rows, stride=half), :] for g in range(group)],
                    axis=0,
                )
                turned.append(
                    lax.dot_general(
                        upside,
                        stacked.astype(jnp.bfloat16),
                        (((1,), (1,)), ((), ())),
                        preferred_element_type=jnp.float32,
                    ).astype(jnp.bfloat16)
                )
            turned_ref[...] = jnp.concatenate(turned, axis=0)
        above, below = (k % group) * rows, LANES - (k % group + 1) * rows
        placed = [ph_ref[pl.ds(k, rows, stride=half), :]]
        if above:
            placed.insert(0, jnp.zeros((above, LANES), jnp.float32))
        if below:
            placed.append(jnp.zeros((below, LANES), jnp.float32))
        products = jnp.dot(
            turned_ref[...],
            jnp.concatenate(placed, axis=0).astype(jnp.bfloat16),
            preferred_element_type=jnp.float32,
        )
        old, mid, new = products[:LANES], products[LANES : 2 * LANES], products[2 * LANES :]
        for ref, total in (
            (lo_ref, jnp.where(band, new, mid)),
            (hi_ref, jnp.where(band, mid, old)),
        ):
            total = pltpu.roll(total, 1, 1, stride=1, stride_axis=0)
            parts = [total[at : at + 8] for at in range(0, LANES, 8)]
            while len(parts) > 1:
                parts = [x + y for x, y in zip(parts[::2], parts[1::2], strict=True)]
            ref[8 * k : 8 * k + 8, :] = parts[0]
    start = pl.multiple_of(core * half, half)
    tiles = [space_ref[pl.ds(start, half), :LANES], space_ref[pl.ds(start, half), LANES : 2 * LANES]]
    for ref in (lo_ref, hi_ref):
        tiles.append(factor * ref[...].reshape(half, 8, LANES).sum(axis=1))
    for t, tile in enumerate(tiles):
        out_ref[t * half : (t + 1) * half, :] = tile
    lane = lax.broadcasted_iota(jnp.int32, (half // 2, LANES), 1)
    rest = space_ref[pl.ds(start, half), 2 * LANES :]
    out_ref[4 * half :, :] = jnp.where(
        lane < HALF, rest[: half // 2], pltpu.roll(rest[half // 2 :], HALF, 1)
    )


def other_half_kernel(
    factor, all_ref, own_ref, xs_ref, signal_ref, other_ref, space_ref, pr_ref, res_ref, *scratch
):
    groups = all_ref.shape[0]
    atoms, wide = space_ref.shape
    channels, samples = signal_ref.shape
    course, patterns = unpacked(all_ref, groups, atoms, samples)
    model = lax.dot_general(
        patterns, course, (((0,), (0,)), ((), ())), preferred_element_type=jnp.float32
    )
    res_ref[channels:, :] = jnp.zeros((wide - channels, samples), jnp.bfloat16)
    res_ref[:channels, :] = (model[:channels] - signal_ref[...].astype(jnp.float32)).astype(
        jnp.bfloat16
    )
    course, patterns = unpacked(own_ref, 1, atoms, samples)
    projected = jnp.dot(patterns, res_ref[...], preferred_element_type=jnp.float32)
    for i in range(samples // LANES):
        pr_ref[i * atoms : (i + 1) * atoms, :] = projected[:, i * LANES : (i + 1) * LANES]
    space_ref[...] = factor * lax.dot_general(
        course, res_ref[...], (((1,), (1,)), ((), ())), preferred_element_type=jnp.float32
    )
    core = lax.axis_index("tm") % 2
    half_of(other_ref, 1 - core, space_ref, xs_ref, pr_ref, *scratch, factor)


def own_half_kernel(factor, space_ref, xs_ref, pr_ref, mine_ref, *scratch):
    core = lax.axis_index("tm") % 2
    half_of(mine_ref, core, space_ref, xs_ref, pr_ref, *scratch, factor)


def outputs_kernel(mine_ref, other_ref, space_ref, time_ref):
    half = space_ref.shape[0] // 2
    channels = space_ref.shape[1]
    core = lax.axis_index("tm") % 2
    for ref, which in ((mine_ref, core), (other_ref, 1 - core)):
        at = pl.multiple_of(which * half, 8)
        tile = [ref[t * half : (t + 1) * half, :] for t in range(4)]
        space_ref[pl.ds(at, half), :LANES] = tile[0]
        space_ref[pl.ds(at, half), LANES : 2 * LANES] = tile[1]
        time_ref[pl.ds(at, half), :LANES] = tile[2]
        time_ref[pl.ds(at, half), LANES:] = tile[3]
        rest = ref[4 * half :, :]
        both = jnp.concatenate([rest, pltpu.roll(rest, HALF, 1)], axis=0)
        space_ref[pl.ds(at, half), 2 * LANES :] = both[:, : channels - 2 * LANES]


def local(signal, spatial, temporal, code_values, block_mask):
    atoms, channels = spatial.shape
    length = temporal.shape[1]
    samples = signal.shape[1]
    groups, slabs = lax.axis_size("atom"), lax.axis_size("tm")
    rows = samples // LANES
    wide = up(channels, LANES)
    factor = 1.0 / math.sqrt(samples * slabs)
    params = pltpu.CompilerParams(vmem_limit_bytes=VMEM_BYTES)

    def swapped(value, bit):
        return lax.ppermute(value, "tm", [(i, i ^ bit) for i in range(slabs)])

    diagonal = pl.pallas_call(
        diagonal_kernel,
        out_shape=jax.ShapeDtypeStruct((atoms, atoms), jnp.float32),
        compiler_params=params,
        cost_estimate=pl.CostEstimate(flops=4_000_000_000, bytes_accessed=8_000_000, transcendentals=0),
        name="diagonal",
    )()
    tail, codes = pl.pallas_call(
        codes_kernel,
        out_shape=(
            jax.ShapeDtypeStruct((atoms, length), jnp.bfloat16),
            jax.ShapeDtypeStruct((rows * atoms, LANES), jnp.float32),
        ),
        compiler_params=params,
        name="codes",
    )(diagonal, code_values, block_mask.T)
    halo = lax.ppermute(tail, "tm", [(i, i + 1) for i in range(slabs - 1)])
    send, xs = pl.pallas_call(
        course_kernel,
        out_shape=(
            jax.ShapeDtypeStruct((groups, (rows + 2) * atoms + atoms // 2, LANES), jnp.bfloat16),
            jax.ShapeDtypeStruct(((rows + length // LANES) * atoms, LANES), jnp.float32),
        ),
        scratch_shapes=[
            pltpu.VMEM((atoms, length), jnp.float32),
            pltpu.VMEM((rows * atoms, LANES), jnp.float32),
        ],
        compiler_params=params,
        name="course",
    )(codes, halo, temporal, spatial)
    everything = lax.all_to_all(send, "atom", split_axis=0, concat_axis=0, tiled=True)
    size = atoms // 2 * 4 + atoms // 4
    half, per = atoms // 2, length // LANES
    share = jax.ShapeDtypeStruct((size, LANES), jnp.float32)
    scratch = [
        pltpu.VMEM(((rows + per) * half, LANES), jnp.float32),
        pltpu.VMEM((rows * half, LANES), jnp.float32),
        pltpu.VMEM((8 * half, LANES), jnp.float32),
        pltpu.VMEM((8 * half, LANES), jnp.float32),
        pltpu.VMEM(((per + 1) * LANES, LANES), jnp.bfloat16),
    ]
    other, space, projected = pl.pallas_call(
        lambda *refs: other_half_kernel(factor, *refs),
        out_shape=(
            share,
            jax.ShapeDtypeStruct((atoms, wide), jnp.float32),
            jax.ShapeDtypeStruct((rows * atoms, LANES), jnp.float32),
        ),
        scratch_shapes=[pltpu.VMEM((wide, samples), jnp.bfloat16), *scratch],
        compiler_params=params,
        name="other_half",
    )(everything, send, xs, signal)
    mine = pl.pallas_call(
        lambda *refs: own_half_kernel(factor, *refs),
        out_shape=share,
        scratch_shapes=scratch,
        compiler_params=params,
        cost_estimate=pl.CostEstimate(flops=200_000_000, bytes_accessed=1_000_000, transcendentals=0),
        name="own_half",
    )(space, xs, projected)
    mine = mine + swapped(other, 1)
    for bit in PARTNERS:
        mine = mine + swapped(mine, bit)
    return pl.pallas_call(
        outputs_kernel,
        out_shape=(
            jax.ShapeDtypeStruct((atoms, channels), jnp.float32),
            jax.ShapeDtypeStruct((atoms, length), jnp.float32),
        ),
        compiler_params=params,
        name="outputs",
    )(mine, swapped(mine, 1))


def solution(mesh):
    in_specs = (P(None, "tm"), P("atom", None), P("atom", None), P("atom", "tm"), P("atom", "tm"))
    out_specs = (P("atom", None), P("atom", None))
    return jax.shard_map(local, mesh=mesh, in_specs=in_specs, out_specs=out_specs, check_vma=False)
```

```python
import math

import jax
import jax.numpy as jnp
from jax import lax
from jax.experimental import pallas as pl
from jax.experimental.pallas import tpu as pltpu
from jax.sharding import PartitionSpec as P

LANES = 128
HALF = LANES // 2
PARTNERS = (4,28,8,2)
VMEM_BYTES = 16 << 20


def up(n, m):
    return -(-n // m) * m


def lower_band(size):
    rows = lax.broadcasted_iota(jnp.int32, (size, size), 0)
    cols = lax.broadcasted_iota(jnp.int32, (size, size), 1)
    return cols >= rows


def diagonal_kernel(out_ref):
    down = lax.broadcasted_iota(jnp.int32, out_ref.shape, 0)
    along = lax.broadcasted_iota(jnp.int32, out_ref.shape, 1)
    out_ref[...] = jnp.where(down == along, 1.0, 0.0)


def codes_kernel(diagonal_ref, cv_ref, mask_ref, tail_ref, own_ref):
    atoms, samples = cv_ref.shape
    length = tail_ref.shape[1]
    per = length // LANES
    for b in reversed(range(samples // length)):
        across = diagonal_ref[...] * mask_ref[b : b + 1, :].astype(jnp.float32)
        on = jnp.sum(across, axis=1, keepdims=True)
        block = cv_ref[:, b * length : (b + 1) * length].astype(jnp.float32) * on
        if (b + 1) * length == samples:
            tail_ref[...] = block.astype(jnp.bfloat16)
        for j in range(per):
            at = (per * b + j) * atoms
            own_ref[at : at + atoms, :] = block[:, j * LANES : (j + 1) * LANES]


def course_kernel(
    own_ref, halo_ref, temporal_ref, spatial_ref, send_ref, xs_ref, tf_ref, cs_ref
):
    copies = send_ref.shape[0]
    atoms, length = temporal_ref.shape
    channels = spatial_ref.shape[1]
    rows = own_ref.shape[0] // atoms
    per = length // LANES
    for j in range(per):
        xs_ref[j * atoms : (j + 1) * atoms, :] = halo_ref[
            :, j * LANES : (j + 1) * LANES
        ].astype(jnp.float32)
    xs_ref[per * atoms :, :] = own_ref[...]
    tf_ref[...] = temporal_ref[...].astype(jnp.float32)
    band = lower_band(LANES)

    def turned(k, at):
        row = tf_ref[k : k + 1, at : at + LANES]
        return pltpu.roll(
            jnp.broadcast_to(row, (LANES, LANES)), 0, 1, stride=1, stride_axis=0
        )

    for k in range(atoms):
        near, far = turned(k, 0), turned(k, LANES)
        matrix = jnp.concatenate(
            [jnp.where(band, 0.0, far), jnp.where(band, far, near), jnp.where(band, near, 0.0)],
            axis=0,
        ).astype(jnp.bfloat16)
        windows = jnp.concatenate(
            [xs_ref[pl.ds(j * atoms + k, rows, stride=atoms), :] for j in range(per + 1)],
            axis=1,
        ).astype(jnp.bfloat16)
        cs_ref[pl.ds(k, rows, stride=atoms), :] = jnp.dot(
            windows, matrix, preferred_element_type=jnp.float32
        )
    rest = jnp.concatenate(
        [
            spatial_ref[:, 2 * LANES :].astype(jnp.float32),
            jnp.zeros((atoms, 3 * LANES - channels), jnp.float32),
        ],
        axis=1,
    )
    tiles = [
        cs_ref[...],
        spatial_ref[:, :LANES],
        spatial_ref[:, LANES : 2 * LANES],
        rest[: atoms // 2] + pltpu.roll(rest[atoms // 2 :], HALF, 1),
    ]
    at = 0
    for tile in tiles:
        for c in range(copies):
            send_ref[c, at : at + tile.shape[0], :] = tile.astype(jnp.bfloat16)
        at += tile.shape[0]


def unpacked(ref, groups, atoms, samples):
    def tile(at):
        return ref[:groups, at : at + atoms, :].reshape(groups * atoms, LANES)

    end = samples // LANES * atoms
    course = jnp.concatenate([tile(at) for at in range(0, end, atoms)], axis=1)
    half = atoms // 2
    rest = ref[:groups, end + 2 * atoms :, :].astype(jnp.float32).reshape(groups * half, LANES)
    lane = lax.broadcasted_iota(jnp.int32, rest.shape, 1)
    sides = [
        jnp.where(lane < HALF, side, 0.0).reshape(groups, half, LANES)
        for side in (rest, pltpu.roll(rest, HALF, 1))
    ]
    last = jnp.concatenate(sides, axis=1).reshape(groups * atoms, LANES).astype(jnp.bfloat16)
    return course, jnp.concatenate([tile(end), tile(end + atoms), last], axis=1)


def half_of(out_ref, core, space_ref, xs_ref, pr_ref, xh_ref, ph_ref, lo_ref, hi_ref, turned_ref, factor):
    atoms = space_ref.shape[0]
    half = atoms // 2
    rows, blocks = pr_ref.shape[0] // atoms, xs_ref.shape[0] // atoms
    for e in range(blocks):
        at = pl.multiple_of(e * atoms + core * half, half)
        xh_ref[e * half : (e + 1) * half, :] = xs_ref[pl.ds(at, half), :]
    for i in range(rows):
        at = pl.multiple_of(i * atoms + core * half, half)
        ph_ref[i * half : (i + 1) * half, :] = pr_ref[pl.ds(at, half), :]
    group = LANES // rows
    down = lax.broadcasted_iota(jnp.int32, (LANES, LANES), 0)
    along = lax.broadcasted_iota(jnp.int32, (LANES, LANES), 1)
    band = along + down >= LANES - 1
    upside = jnp.where(along + down == LANES - 1, 1.0, 0.0).astype(jnp.bfloat16)
    for k in range(half):
        if k % group == 0:
            turned = []
            for j in range(3):
                stacked = jnp.concatenate(
                    [xh_ref[pl.ds(j * half + k + g, rows, stride=half), :] for g in range(group)],
                    axis=0,
                )
                turned.append(
                    lax.dot_general(
                        upside,
                        stacked.astype(jnp.bfloat16),
                        (((1,), (1,)), ((), ())),
                        preferred_element_type=jnp.float32,
                    ).astype(jnp.bfloat16)
                )
            turned_ref[...] = jnp.concatenate(turned, axis=0)
        above, below = (k % group) * rows, LANES - (k % group + 1) * rows
        placed = [ph_ref[pl.ds(k, rows, stride=half), :]]
        if above:
            placed.insert(0, jnp.zeros((above, LANES), jnp.float32))
        if below:
            placed.append(jnp.zeros((below, LANES), jnp.float32))
        products = jnp.dot(
            turned_ref[...],
            jnp.concatenate(placed, axis=0).astype(jnp.bfloat16),
            preferred_element_type=jnp.float32,
        )
        old, mid, new = products[:LANES], products[LANES : 2 * LANES], products[2 * LANES :]
        for ref, total in (
            (lo_ref, jnp.where(band, new, mid)),
            (hi_ref, jnp.where(band, mid, old)),
        ):
            total = pltpu.roll(total, 1, 1, stride=1, stride_axis=0)
            parts = [total[at : at + 8] for at in range(0, LANES, 8)]
            while len(parts) > 1:
                parts = [x + y for x, y in zip(parts[::2], parts[1::2], strict=True)]
            ref[8 * k : 8 * k + 8, :] = parts[0]
    start = pl.multiple_of(core * half, half)
    tiles = [space_ref[pl.ds(start, half), :LANES], space_ref[pl.ds(start, half), LANES : 2 * LANES]]
    for ref in (lo_ref, hi_ref):
        tiles.append(factor * ref[...].reshape(half, 8, LANES).sum(axis=1))
    for t, tile in enumerate(tiles):
        out_ref[t * half : (t + 1) * half, :] = tile
    lane = lax.broadcasted_iota(jnp.int32, (half // 2, LANES), 1)
    rest = space_ref[pl.ds(start, half), 2 * LANES :]
    out_ref[4 * half :, :] = jnp.where(
        lane < HALF, rest[: half // 2], pltpu.roll(rest[half // 2 :], HALF, 1)
    )


def other_half_kernel(
    factor, all_ref, own_ref, xs_ref, signal_ref, other_ref, space_ref, pr_ref, res_ref, *scratch
):
    groups = all_ref.shape[0]
    atoms, wide = space_ref.shape
    channels, samples = signal_ref.shape
    course, patterns = unpacked(all_ref, groups, atoms, samples)
    model = lax.dot_general(
        patterns, course, (((0,), (0,)), ((), ())), preferred_element_type=jnp.float32
    )
    res_ref[channels:, :] = jnp.zeros((wide - channels, samples), jnp.bfloat16)
    res_ref[:channels, :] = (model[:channels] - signal_ref[...].astype(jnp.float32)).astype(
        jnp.bfloat16
    )
    course, patterns = unpacked(own_ref, 1, atoms, samples)
    projected = jnp.dot(patterns, res_ref[...], preferred_element_type=jnp.float32)
    for i in range(samples // LANES):
        pr_ref[i * atoms : (i + 1) * atoms, :] = projected[:, i * LANES : (i + 1) * LANES]
    space_ref[...] = factor * lax.dot_general(
        course, res_ref[...], (((1,), (1,)), ((), ())), preferred_element_type=jnp.float32
    )
    core = lax.axis_index("tm") % 2
    half_of(other_ref, 1 - core, space_ref, xs_ref, pr_ref, *scratch, factor)


def own_half_kernel(factor, space_ref, xs_ref, pr_ref, mine_ref, *scratch):
    core = lax.axis_index("tm") % 2
    half_of(mine_ref, core, space_ref, xs_ref, pr_ref, *scratch, factor)


def outputs_kernel(mine_ref, other_ref, space_ref, time_ref):
    half = space_ref.shape[0] // 2
    channels = space_ref.shape[1]
    core = lax.axis_index("tm") % 2
    for ref, which in ((mine_ref, core), (other_ref, 1 - core)):
        at = pl.multiple_of(which * half, 8)
        tile = [ref[t * half : (t + 1) * half, :] for t in range(4)]
        space_ref[pl.ds(at, half), :LANES] = tile[0]
        space_ref[pl.ds(at, half), LANES : 2 * LANES] = tile[1]
        time_ref[pl.ds(at, half), :LANES] = tile[2]
        time_ref[pl.ds(at, half), LANES:] = tile[3]
        rest = ref[4 * half :, :]
        both = jnp.concatenate([rest, pltpu.roll(rest, HALF, 1)], axis=0)
        space_ref[pl.ds(at, half), 2 * LANES :] = both[:, : channels - 2 * LANES]


def local(signal, spatial, temporal, code_values, block_mask):
    atoms, channels = spatial.shape
    length = temporal.shape[1]
    samples = signal.shape[1]
    groups, slabs = lax.axis_size("atom"), lax.axis_size("tm")
    rows = samples // LANES
    wide = up(channels, LANES)
    factor = 1.0 / math.sqrt(samples * slabs)
    params = pltpu.CompilerParams(vmem_limit_bytes=VMEM_BYTES)

    def swapped(value, bit):
        return lax.ppermute(value, "tm", [(i, i ^ bit) for i in range(slabs)])

    diagonal = pl.pallas_call(
        diagonal_kernel,
        out_shape=jax.ShapeDtypeStruct((atoms, atoms), jnp.float32),
        compiler_params=params,
        cost_estimate=pl.CostEstimate(flops=4_000_000_000, bytes_accessed=8_000_000, transcendentals=0),
        name="diagonal",
    )()
    tail, codes = pl.pallas_call(
        codes_kernel,
        out_shape=(
            jax.ShapeDtypeStruct((atoms, length), jnp.bfloat16),
            jax.ShapeDtypeStruct((rows * atoms, LANES), jnp.float32),
        ),
        compiler_params=params,
        name="codes",
    )(diagonal, code_values, block_mask.T)
    halo = lax.ppermute(tail, "tm", [(i, i + 1) for i in range(slabs - 1)])
    send, xs = pl.pallas_call(
        course_kernel,
        out_shape=(
            jax.ShapeDtypeStruct((groups, (rows + 2) * atoms + atoms // 2, LANES), jnp.bfloat16),
            jax.ShapeDtypeStruct(((rows + length // LANES) * atoms, LANES), jnp.float32),
        ),
        scratch_shapes=[
            pltpu.VMEM((atoms, length), jnp.float32),
            pltpu.VMEM((rows * atoms, LANES), jnp.float32),
        ],
        compiler_params=params,
        name="course",
    )(codes, halo, temporal, spatial)
    everything = lax.all_to_all(send, "atom", split_axis=0, concat_axis=0, tiled=True)
    size = atoms // 2 * 4 + atoms // 4
    half, per = atoms // 2, length // LANES
    share = jax.ShapeDtypeStruct((size, LANES), jnp.float32)
    scratch = [
        pltpu.VMEM(((rows + per) * half, LANES), jnp.float32),
        pltpu.VMEM((rows * half, LANES), jnp.float32),
        pltpu.VMEM((8 * half, LANES), jnp.float32),
        pltpu.VMEM((8 * half, LANES), jnp.float32),
        pltpu.VMEM(((per + 1) * LANES, LANES), jnp.bfloat16),
    ]
    other, space, projected = pl.pallas_call(
        lambda *refs: other_half_kernel(factor, *refs),
        out_shape=(
            share,
            jax.ShapeDtypeStruct((atoms, wide), jnp.float32),
            jax.ShapeDtypeStruct((rows * atoms, LANES), jnp.float32),
        ),
        scratch_shapes=[pltpu.VMEM((wide, samples), jnp.bfloat16), *scratch],
        compiler_params=params,
        name="other_half",
    )(everything, send, xs, signal)
    mine = pl.pallas_call(
        lambda *refs: own_half_kernel(factor, *refs),
        out_shape=share,
        scratch_shapes=scratch,
        compiler_params=params,
        cost_estimate=pl.CostEstimate(flops=200_000_000, bytes_accessed=1_000_000, transcendentals=0),
        name="own_half",
    )(space, xs, projected)
    mine = mine + swapped(other, 1)
    for bit in PARTNERS:
        mine = mine + swapped(mine, bit)
    return pl.pallas_call(
        outputs_kernel,
        out_shape=(
            jax.ShapeDtypeStruct((atoms, channels), jnp.float32),
            jax.ShapeDtypeStruct((atoms, length), jnp.float32),
        ),
        compiler_params=params,
        name="outputs",
    )(mine, swapped(mine, 1))


def solution(mesh):
    in_specs = (P(None, "tm"), P("atom", None), P("atom", None), P("atom", "tm"), P("atom", "tm"))
    out_specs = (P("atom", None), P("atom", None))
    return jax.shard_map(local, mesh=mesh, in_specs=in_specs, out_specs=out_specs, check_vma=False)
```
